32 devices in a mesh: orb: 8 (over y, x, core), slab: 4 (over z).
Axes of the slice: x: 2, y: 2, z: 4, core: 2. Of those that a mesh axis runs over, the one named last changes fastest.
Arguments:
- pool: float32 [16, 32, 32, 128], P('orb', 'slab'), may hold values from -6 to 6
- target_row: int32 [8], P('orb'), may hold values from 0 to 1
- source_index: int32 [3], replicated, may hold values from 0 to 15
- metric: float32 [3, 32, 32, 128], P(None, 'slab'), may hold values from 0.3 to 3
- screening: float32 [32, 32, 128], P('slab'), may hold values from 0.05 to 4
Outputs:
- exchange: float32 [8, 32, 32, 128], P('orb', 'slab')
The draws below stay inside these ranges and needn't reach their ends.
All inputs are finite; a program needn't handle non-finite values.
Results may differ from the reference program's by a relative error of at most 0.000096.
Values sent between devices are 32-bit elements; how exact they have to be, the bound alone decides.
No kernel may reach another device: no remote copies, remote signals or barrier semaphores. Data moves between devices by JAX's collectives and lax.ppermute only.
A program may use at most 64 MiB of HBM per device.

```python
import math
import jax
import jax.numpy as jnp
from jax import lax

GX = 32
GY = 128
SRC_DEV = 2
TGT_DEV = 1
NSRC = 3
SWEEPS = 6
NZ = 32
POOL = 16
TARGETS = 8


def set_ends(values, rng, smallest, largest):
    place = [jax.random.randint(jax.random.fold_in(rng, axis), (), 0, length) for axis, length in enumerate(values.shape)]
    longest = values.shape.index(max(values.shape))
    beside = place[:longest] + [(place[longest] + 1) % values.shape[longest]] + place[longest + 1:]
    return values.at[tuple(place)].set(smallest).at[tuple(beside)].set(largest)


def block_levels(key, dims, pieces, low, top_value):
    def one(dim, blocks):
        draws = jax.random.uniform(jax.random.fold_in(jax.random.fold_in(key, 6), dim), (blocks,), jnp.float32, low / len(pieces), top_value / len(pieces))
        return jnp.repeat(jnp.exp(draws), dims[dim] // blocks).reshape((-1,) + (1,) * (len(dims) - dim - 1))

    level = one(*pieces[0])
    for cut in pieces[1:]:
        level = level * one(*cut)
    return level


def normal_values(key, extent, scale, reach, pieces=(), kind=jnp.bfloat16):
    loudness = block_levels(key, extent, pieces, -0.22, 0.18) if pieces else 1.0
    array = jax.random.normal(key, extent, jnp.float32) * scale * loudness
    return jnp.minimum(jnp.maximum(array, -reach), reach).astype(kind)


def setup_inputs(seed: int = 0) -> dict:
    arg_keys = jax.random.split(jax.random.key(seed), 6)
    return {
        "pool": normal_values(arg_keys[0], (POOL, NZ, GX, GY), 1.0, 6.0, ((0, 8), (1, 4)), jnp.float32),
        "target_row": set_ends(jax.random.randint(arg_keys[1], (TARGETS,), 0, SRC_DEV), jax.random.fold_in(arg_keys[1], 1), 0, SRC_DEV - 1).astype(jnp.int32),
        "source_index": jax.random.randint(arg_keys[2], (NSRC,), 0, POOL).astype(jnp.int32),
        "metric": jnp.clip(jnp.exp(math.log(3.0) - 2.3025851 * jax.random.uniform(arg_keys[3], (3, NZ, GX, GY), jnp.float32) ** block_levels(arg_keys[3], (3, NZ, GX, GY), ((1, 4),), -0.2, 0.2)), 0.3, 3.0),
        "screening": jnp.clip(jnp.exp(math.log(4.0) - 4.3820266 * jax.random.uniform(arg_keys[4], (NZ, GX, GY), jnp.float32) ** block_levels(arg_keys[4], (NZ, GX, GY), ((0, 4),), -0.2, 0.2)), 0.05, 4.0),
    }


def lower_z(f):
    return jnp.concatenate([jnp.zeros_like(f[..., :1, :, :]), f[..., :-1, :, :]], axis=-3)


def upper_z(f):
    return jnp.concatenate([f[..., 1:, :, :], jnp.zeros_like(f[..., :1, :, :])], axis=-3)


def lower_x(f):
    return jnp.concatenate([jnp.zeros_like(f[..., :1, :]), f[..., :-1, :]], axis=-2)


def upper_x(f):
    return jnp.concatenate([f[..., 1:, :], jnp.zeros_like(f[..., :1, :])], axis=-2)


def lower_y(f):
    return jnp.concatenate([jnp.zeros_like(f[..., :1]), f[..., :-1]], axis=-1)


def upper_y(f):
    return jnp.concatenate([f[..., 1:], jnp.zeros_like(f[..., :1])], axis=-1)


def step_sizes(count):
    return [1.0 / (1.025 + 0.975 * math.cos(math.pi * (2 * k + 1) / (2 * count))) for k in range(count)]


def reference(pool, target_row, source_index, metric, screening):
    face_x, face_y, face_z = metric[0], metric[1], metric[2]
    below_x, below_y, below_z = lower_x(face_x), lower_y(face_y), lower_z(face_z)
    diag = screening + face_z + below_z + face_x + below_x + face_y + below_y
    sources = jnp.take(pool, source_index, axis=0)
    groups = jnp.arange(TARGETS, dtype=jnp.int32) // TGT_DEV
    rows = (groups * SRC_DEV + target_row).astype(jnp.int32)
    targets = jnp.take(pool, rows, axis=0)
    weights = step_sizes(SWEEPS)

    def solve_one(target):
        density = target[None] * sources
        field = weights[0] * density / diag
        for k in range(1, SWEEPS):
            image = (diag * field - face_z * upper_z(field) - below_z * lower_z(field)
                     - face_x * upper_x(field) - below_x * lower_x(field)
                     - face_y * upper_y(field) - below_y * lower_y(field))
            field = field + weights[k] * (density - image) / diag
        return jnp.sum(field * sources, axis=0)

    return lax.map(solve_one, targets)
```

```python
import functools
import math

import jax
import jax.numpy as jnp
from jax import lax
from jax.experimental import pallas as pl
from jax.experimental.pallas import tpu as pltpu
from jax.sharding import PartitionSpec as P

NSRC = 3
SWEEPS = 6
HALO = SWEEPS - 1
AXES = ("orb", "slab")
VMEM = pl.BlockSpec(memory_space=pltpu.VMEM)
SMEM = pl.BlockSpec(memory_space=pltpu.SMEM)


def step_sizes(count):
    return [
        1.0 / (1.025 + 0.975 * math.cos(math.pi * (2 * k + 1) / (2 * count))) for k in range(count)
    ]


def call(kernel, out_shapes, in_specs, scratch=(), flops=0, moved=0):
    return pl.pallas_call(
        kernel,
        out_shape=[jax.ShapeDtypeStruct(s, jnp.float32) for s in out_shapes],
        in_specs=in_specs,
        out_specs=[VMEM] * len(out_shapes),
        scratch_shapes=list(scratch),
        compiler_params=pltpu.CompilerParams(vmem_limit_bytes=16 << 20),
        cost_estimate=pl.CostEstimate(flops=flops, transcendentals=0, bytes_accessed=moved),
    )


def pick_kernel(where, index, row, pool, send, own):
    orb, core = where[0], where[1]
    held, planes = pool.shape[0], pool.shape[1]
    mine = core * (planes - HALO)
    other = (1 - core) * (planes - HALO)
    for out, start in ((send, other), (own, mine)):
        for s in range(NSRC):
            held_here = index[s] // held == orb
            cells = pool[index[s] % held, pl.ds(start, HALO)]
            out[s] = jnp.where(held_here, cells, 0.0)
        out[NSRC] = pool[row[0], pl.ds(start, HALO)]


def coefficient_kernel(
    where, row, pool, metric, screening, near, far, coef, scaled, fx, fy, fz, scr, tgt
):
    core, slab, slabs = where[1], where[2], where[3]
    planes, gx, gy = screening.shape
    total = planes + 2 * HALO
    lower = core * (HALO + planes)
    upper = (1 - core) * (HALO + planes)
    h = HALO
    for halo, at, own_slot in ((near, lower, 5 * h + 1), (far, upper, 4 * h + 1)):
        scr[pl.ds(at, h)] = halo[0:h]
        fx[pl.ds(at, h)] = halo[h : 2 * h]
        fy[pl.ds(at, h)] = halo[2 * h : 3 * h]
        tgt[pl.ds(at, h)] = halo[own_slot : own_slot + h]
    low_z = jnp.where(core == 0, near[3 * h : 4 * h + 1], far[3 * h : 4 * h + 1])
    high_z = jnp.where(core == 0, far[3 * h : 4 * h], near[3 * h : 4 * h])
    fz[0 : h + 1] = low_z
    fz[h + 1 : h + 1 + planes] = metric[2]
    fz[h + 1 + planes :] = high_z
    scr[h : h + planes] = screening[...]
    fx[h : h + planes] = metric[0]
    fy[h : h + planes] = metric[1]
    tgt[h : h + planes] = pool[row[0]]
    first = jnp.where(slab == 0, h, 0)
    last = jnp.where(slab == slabs - 1, h + planes, total)
    x_id = lax.broadcasted_iota(jnp.int32, (gx, gy), 0)
    y_id = lax.broadcasted_iota(jnp.int32, (gx, gy), 1)

    @pl.loop(0, total)
    def _(e):
        z_hi, z_lo = fz[e + 1], fz[e]
        x_hi, y_hi = fx[e], fy[e]
        x_lo = jnp.where(x_id == 0, 0.0, pltpu.roll(x_hi, 1, 0))
        y_lo = jnp.where(y_id == 0, 0.0, pltpu.roll(y_hi, 1, 1))
        diag = scr[e] + z_hi + z_lo + x_hi + x_lo + y_hi + y_lo
        inside = jnp.logical_and(e >= first, e < last)
        inverse = 1.0 / jnp.where(inside, diag, 1.0)
        inverse = jnp.where(inside, inverse, 0.0)
        rows = pl.ds(pl.multiple_of(e * gx, gx), gx)
        coef[0, rows] = z_hi * inverse
        coef[1, rows] = z_lo * inverse
        coef[2, rows] = jnp.where(x_id == gx - 1, 0.0, x_hi * inverse)
        coef[3, rows] = x_lo * inverse
        coef[4, rows] = jnp.where(y_id == gy - 1, 0.0, y_hi * inverse)
        coef[5, rows] = y_lo * inverse
        scaled[rows] = tgt[e] * inverse


def sweep_kernel(weights, where, coef, scaled, middle, halo, sibling, out, src, base, ping, pong):
    core = where[1]
    h = HALO
    gx, gy = out.shape[-2:]
    planes = out.shape[1]
    total = planes + 2 * h
    extra = middle.shape[1]
    kept = planes
    halo_at = core * (h + planes)
    middle_at = h + core * (planes - extra)
    sibling_at = (1 - core) * (h + extra)
    for part, at in ((halo, halo_at), (middle, middle_at), (sibling, sibling_at)):
        count = part.shape[1]
        for s in range(NSRC):
            src[s, pl.ds(pl.multiple_of(at * gx, gx), count * gx)] = part[s].reshape(count * gx, gy)

    @pl.loop(0, total)
    def _(e):
        rows = pl.ds(pl.multiple_of(e * gx, gx), gx)
        t = scaled[rows]
        for s in range(NSRC):
            b = t * src[s, rows]
            base[s, rows] = b
            ping[s, rows] = weights[0] * b

    old, new = ping, pong
    for k in range(1, SWEEPS):
        w = weights[k]
        lastly = k == SWEEPS - 1

        @pl.loop(k, total - k)
        def _(e):
            start = pl.multiple_of(e * gx, gx)
            for j in range(0, gx, 8):
                at = start + j
                rows = pl.ds(at, 8)
                c = [coef[i, rows] for i in range(6)]
                acc = None
                for s in range(NSRC):
                    v = old[s, rows]
                    total_s = base[s, rows]
                    total_s += c[0] * old[s, pl.ds(at + gx, 8)]
                    total_s += c[1] * old[s, pl.ds(at - gx, 8)]
                    total_s += c[2] * old[s, pl.ds(at + 1, 8)]
                    total_s += c[3] * old[s, pl.ds(at - 1, 8)]
                    total_s += c[4] * pltpu.roll(v, gy - 1, 1)
                    total_s += c[5] * pltpu.roll(v, 1, 1)
                    v = (1.0 - w) * v + w * total_s
                    if lastly:
                        term = v * src[s, rows]
                        acc = term if acc is None else acc + term
                    else:
                        new[s, rows] = v
                if lastly:
                    out[0, e - h, j : j + 8] = acc

        old, new = new, old


def shards(pool, target_row, source_index, metric, screening):
    held, planes, gx, gy = pool.shape
    n_orb, n_slab = lax.axis_size("orb"), lax.axis_size("slab")
    h = HALO
    weights = step_sizes(SWEEPS)
    orb, slab = lax.axis_index("orb"), lax.axis_index("slab")
    core = orb % 2
    where = jnp.stack([orb, core, slab, jnp.int32(n_slab)])

    def place(o, z):
        return o * n_slab + z

    def among(moved):
        pairs = [
            (place(o, z), place(*moved(o, z)))
            for o in range(n_orb)
            for z in range(n_slab)
            if 0 <= moved(o, z)[1] < n_slab
        ]
        return lambda x: lax.ppermute(x, AXES, pairs)

    to_sibling = among(lambda o, z: (o ^ 1, z))
    to_slab = among(lambda o, z: (o ^ 1, z + 1 if o % 2 else z - 1))
    bits = [1 << b for b in range(1, n_orb.bit_length() - 1)]

    send, own = call(
        pick_kernel,
        [(NSRC + 1, h, gx, gy)] * 2,
        [SMEM, SMEM, SMEM, VMEM],
    )(where, source_index, target_row, pool)
    got = to_sibling(send)
    part = own[:NSRC] + got[:NSRC]
    start = core * (planes - h)
    near_z = core * (planes - h - 1)
    half = functools.partial(lax.dynamic_slice_in_dim, start_index=start, slice_size=h, axis=0)
    edge = jnp.concatenate(
        [
            half(screening),
            half(metric[0]),
            half(metric[1]),
            lax.dynamic_slice_in_dim(metric[2], near_z, h + 1, axis=0),
            own[NSRC],
            got[NSRC],
        ],
        axis=0,
    )
    near = to_slab(edge)
    for low, high in zip(bits, reversed(bits)):
        part = part + among(lambda o, z: (o ^ (high if o % 2 else low), z))(part)
    halo = to_slab(part)
    far = to_sibling(near[: 5 * h + 1])
    kept = planes - h
    lacks = jnp.where(
        core == 0,
        jnp.concatenate([halo, part[:, :kept]], axis=1),
        jnp.concatenate([part[:, h - kept :], halo], axis=1),
    )
    sibling = to_sibling(lacks)
    total = planes + 2 * h
    coef, scaled = call(
        coefficient_kernel,
        [(6, total * gx, gy), (total * gx, gy)],
        [SMEM, SMEM] + [VMEM] * 5,
        [pltpu.VMEM((total, gx, gy), jnp.float32)] * 2
        + [pltpu.VMEM((total + 1, gx, gy), jnp.float32)]
        + [pltpu.VMEM((total, gx, gy), jnp.float32)] * 2,
    )(where, target_row, pool, metric, screening, near, far)
    field = pltpu.VMEM((NSRC, total * gx, gy), jnp.float32)
    (out,) = call(
        functools.partial(sweep_kernel, weights),
        [(1, planes, gx, gy)],
        [SMEM] + [VMEM] * 5,
        [field] * 4,
    )(where, coef, scaled, part, halo, sibling)
    return out


def solution(mesh):
    in_specs = (
        P("orb", "slab", None, None),
        P("orb"),
        P(),
        P(None, "slab", None, None),
        P("slab", None, None),
    )
    out_specs = P("orb", "slab", None, None)
    return jax.shard_map(shards, mesh=mesh, in_specs=in_specs, out_specs=out_specs, check_vma=False)
```

```python
import functools
import math

import jax
import jax.numpy as jnp
from jax import lax
from jax.experimental import pallas as pl
from jax.experimental.pallas import tpu as pltpu
from jax.sharding import PartitionSpec as P

NSRC = 3
SWEEPS = 6
HALO = SWEEPS - 1
AXES = ("orb", "slab")
VMEM = pl.BlockSpec(memory_space=pltpu.VMEM)
SMEM = pl.BlockSpec(memory_space=pltpu.SMEM)
HBM = pl.BlockSpec(memory_space=pltpu.HBM)


def step_sizes(count):
    return [
        1.0 / (1.025 + 0.975 * math.cos(math.pi * (2 * k + 1) / (2 * count))) for k in range(count)
    ]


def call(kernel, out_shapes, in_specs, scratch=(), flops=0, moved=0):
    return pl.pallas_call(
        kernel,
        out_shape=[jax.ShapeDtypeStruct(s, jnp.float32) for s in out_shapes],
        in_specs=in_specs,
        out_specs=[VMEM] * len(out_shapes),
        scratch_shapes=list(scratch),
        compiler_params=pltpu.CompilerParams(vmem_limit_bytes=16 << 20),
        cost_estimate=pl.CostEstimate(flops=flops, transcendentals=0, bytes_accessed=moved),
    )


def pick_kernel(
    row, index_hbm, pool_hbm, metric_hbm, screening_hbm,
    send, own, edge, target, index, pool, sems,
):
    h = HALO
    held, planes = pool.shape[0], pool.shape[1]
    orb = lax.axis_index("orb")
    core = lax.rem(orb, 2)
    mine = core * (planes - h)
    other = (1 - core) * (planes - h)
    parts = [
        (index_hbm, index),
        (pool_hbm, pool),
        (screening_hbm.at[pl.ds(mine, h)], edge.at[pl.ds(0, h)]),
        (metric_hbm.at[0, pl.ds(mine, h)], edge.at[pl.ds(h, h)]),
        (metric_hbm.at[1, pl.ds(mine, h)], edge.at[pl.ds(2 * h, h)]),
        (
            metric_hbm.at[2, pl.ds(core * (planes - h - 1), h + 1)],
            edge.at[pl.ds(3 * h, h + 1)],
        ),
    ]
    copies = [pltpu.make_async_copy(a, b, sems.at[i]) for i, (a, b) in enumerate(parts)]
    for copy in copies:
        copy.start()
    for copy in copies[:2]:
        copy.wait()
    for out, start in ((send, other), (own, mine)):
        for s in range(NSRC):
            held_here = index[s] // held == orb
            cells = pool[lax.rem(index[s], held), pl.ds(start, h)]
            out[s] = jnp.where(held_here, cells, 0.0)
        out[NSRC] = pool[row[0], pl.ds(start, h)]
    target[...] = pool[row[0]]
    edge[pl.ds(4 * h + 1, h)] = pool[row[0], pl.ds(mine, h)]
    edge[pl.ds(5 * h + 1, h)] = jnp.zeros((h,) + edge.shape[1:], jnp.float32)
    for copy in copies[2:]:
        copy.wait()


def coefficient_kernel(
    target, metric, screening, near, far, coef, scaled, fx, fy, fz, scr, tgt
):
    core = lax.rem(lax.axis_index("orb"), 2)
    slab, slabs = lax.axis_index("slab"), lax.axis_size("slab")
    planes, gx, gy = screening.shape
    total = planes + 2 * HALO
    lower = core * (HALO + planes)
    upper = (1 - core) * (HALO + planes)
    h = HALO
    for halo, at, own_slot in ((near, lower, 5 * h + 1), (far, upper, 4 * h + 1)):
        scr[pl.ds(at, h)] = halo[0:h]
        fx[pl.ds(at, h)] = halo[h : 2 * h]
        fy[pl.ds(at, h)] = halo[2 * h : 3 * h]
        tgt[pl.ds(at, h)] = halo[own_slot : own_slot + h]
    low_z = jnp.where(core == 0, near[3 * h : 4 * h + 1], far[3 * h : 4 * h + 1])
    high_z = jnp.where(core == 0, far[3 * h : 4 * h], near[3 * h : 4 * h])
    fz[0 : h + 1] = low_z
    fz[h + 1 : h + 1 + planes] = metric[2]
    fz[h + 1 + planes :] = high_z
    scr[h : h + planes] = screening[...]
    fx[h : h + planes] = metric[0]
    fy[h : h + planes] = metric[1]
    tgt[h : h + planes] = target[...]
    first = jnp.where(slab == 0, h, 0)
    last = jnp.where(slab == slabs - 1, h + planes, total)
    x_id = lax.broadcasted_iota(jnp.int32, (gx, gy), 0)
    y_id = lax.broadcasted_iota(jnp.int32, (gx, gy), 1)

    @pl.loop(0, total)
    def _(e):
        z_hi, z_lo = fz[e + 1], fz[e]
        x_hi, y_hi = fx[e], fy[e]
        x_lo = jnp.where(x_id == 0, 0.0, pltpu.roll(x_hi, 1, 0))
        y_lo = jnp.where(y_id == 0, 0.0, pltpu.roll(y_hi, 1, 1))
        diag = scr[e] + z_hi + z_lo + x_hi + x_lo + y_hi + y_lo
        inside = jnp.logical_and(e >= first, e < last)
        inverse = 1.0 / jnp.where(inside, diag, 1.0)
        inverse = jnp.where(inside, inverse, 0.0)
        rows = pl.ds(pl.multiple_of(e * gx, gx), gx)
        coef[0, rows] = z_hi * inverse
        coef[1, rows] = z_lo * inverse
        coef[2, rows] = jnp.where(x_id == gx - 1, 0.0, x_hi * inverse)
        coef[3, rows] = x_lo * inverse
        coef[4, rows] = jnp.where(y_id == gy - 1, 0.0, y_hi * inverse)
        coef[5, rows] = y_lo * inverse
        scaled[rows] = tgt[e] * inverse


def sweep_kernel(weights, coef, scaled, middle, halo, sibling, out, src, base, ping, pong):
    core = lax.rem(lax.axis_index("orb"), 2)
    h = HALO
    gx, gy = out.shape[-2:]
    planes = out.shape[1]
    total = planes + 2 * h
    extra = middle.shape[1]
    halo_at = core * (h + planes)
    middle_at = h + core * (planes - extra)
    sibling_at = (1 - core) * (h + extra)
    for part, at in ((halo, halo_at), (middle, middle_at), (sibling, sibling_at)):
        count = part.shape[1]
        for s in range(NSRC):
            src[s, pl.ds(pl.multiple_of(at * gx, gx), count * gx)] = part[s].reshape(count * gx, gy)

    @pl.loop(0, total)
    def _(e):
        rows = pl.ds(pl.multiple_of(e * gx, gx), gx)
        t = scaled[rows]
        for s in range(NSRC):
            b = t * src[s, rows]
            base[s, rows] = b
            ping[s, rows] = weights[0] * b

    old, new = ping, pong
    for k in range(1, SWEEPS):
        w = weights[k]
        lastly = k == SWEEPS - 1

        @pl.loop(k, total - k, unroll=4)
        def _(e):
            start = pl.multiple_of(e * gx, gx)
            for j in range(0, gx, 8):
                at = start + j
                rows = pl.ds(at, 8)
                c = [coef[i, rows] for i in range(6)]
                acc = None
                for s in range(NSRC):
                    v = old[s, rows]
                    total_s = base[s, rows]
                    total_s += c[0] * old[s, pl.ds(at + gx, 8)]
                    total_s += c[1] * old[s, pl.ds(at - gx, 8)]
                    total_s += c[2] * old[s, pl.ds(at + 1, 8)]
                    total_s += c[3] * old[s, pl.ds(at - 1, 8)]
                    total_s += c[4] * pltpu.roll(v, gy - 1, 1)
                    total_s += c[5] * pltpu.roll(v, 1, 1)
                    v = (1.0 - w) * v + w * total_s
                    if lastly:
                        term = v * src[s, rows]
                        acc = term if acc is None else acc + term
                    else:
                        new[s, rows] = v
                if lastly:
                    out[0, e - h, j : j + 8] = acc

        old, new = new, old


def shards(pool, target_row, source_index, metric, screening):
    held, planes, gx, gy = pool.shape
    n_orb, n_slab = lax.axis_size("orb"), lax.axis_size("slab")
    h = HALO
    weights = step_sizes(SWEEPS)
    core = lax.axis_index("orb") % 2

    def place(o, z):
        return o * n_slab + z

    def among(moved):
        pairs = [
            (place(o, z), place(*moved(o, z)))
            for o in range(n_orb)
            for z in range(n_slab)
            if 0 <= moved(o, z)[1] < n_slab
        ]
        return lambda x: lax.ppermute(x, AXES, pairs)

    to_sibling = among(lambda o, z: (o ^ 1, z))
    to_slab = among(lambda o, z: (o ^ 1, z + 1 if o % 2 else z - 1))
    bits = [1 << b for b in range(1, n_orb.bit_length() - 1)]

    send, own, edge, target = call(
        pick_kernel,
        [(NSRC + 1, h, gx, gy)] * 2 + [(6 * h + 1, gx, gy), (planes, gx, gy)],
        [SMEM] + [HBM] * 4,
        [
            pltpu.SMEM(source_index.shape, jnp.int32),
            pltpu.VMEM(pool.shape, jnp.float32),
            pltpu.SemaphoreType.DMA((6,)),
        ],
        moved=4 << 20,
    )(target_row, *[pltpu.with_memory_space_constraint(x, pltpu.HBM) for x in (source_index, pool, metric, screening)])
    got = to_sibling(send)
    part = own[:NSRC] + got[:NSRC]
    edge = edge.at[5 * h + 1 :].set(got[NSRC])
    near = to_slab(edge)
    for low, high in zip(bits, reversed(bits)):
        part = part + among(lambda o, z: (o ^ (high if o % 2 else low), z))(part)
    halo = to_slab(part)
    far = to_sibling(near[: 5 * h + 1])
    total = planes + 2 * h
    coef, scaled = call(
        coefficient_kernel,
        [(6, total * gx, gy), (total * gx, gy)],
        [VMEM] * 5,
        [pltpu.VMEM((total, gx, gy), jnp.float32)] * 2
        + [pltpu.VMEM((total + 1, gx, gy), jnp.float32)]
        + [pltpu.VMEM((total, gx, gy), jnp.float32)] * 2,
        moved=8 << 20,
    )(target, metric, screening, near, far)
    halo, coef, scaled = lax.optimization_barrier((halo, coef, scaled))
    kept = planes - h
    lacks = jnp.where(
        core == 0,
        jnp.concatenate([halo, part[:, :kept]], axis=1),
        jnp.concatenate([part[:, h - kept :], halo], axis=1),
    )
    sibling = to_sibling(lacks)
    field = pltpu.VMEM((NSRC, total * gx, gy), jnp.float32)
    (out,) = call(
        functools.partial(sweep_kernel, weights),
        [(1, planes, gx, gy)],
        [VMEM] * 5,
        [field] * 4,
        moved=12 << 20,
    )(coef, scaled, part, halo, sibling)
    return out


def solution(mesh):
    in_specs = (
        P("orb", "slab", None, None),
        P("orb"),
        P(),
        P(None, "slab", None, None),
        P("slab", None, None),
    )
    out_specs = P("orb", "slab", None, None)
    return jax.shard_map(shards, mesh=mesh, in_specs=in_specs, out_specs=out_specs, check_vma=False)
```

```python
import functools
import math

import jax
import jax.numpy as jnp
from jax import lax
from jax.experimental import pallas as pl
from jax.experimental.pallas import tpu as pltpu
from jax.sharding import PartitionSpec as P

NSRC = 3
SWEEPS = 6
HALO = SWEEPS - 1
AXES = ("orb", "slab")
HINT = 10**9
VMEM = pl.BlockSpec(memory_space=pltpu.VMEM)
SMEM = pl.BlockSpec(memory_space=pltpu.SMEM)
HBM = pl.BlockSpec(memory_space=pltpu.HBM)


def step_sizes(count):
    return [
        1.0 / (1.025 + 0.975 * math.cos(math.pi * (2 * k + 1) / (2 * count))) for k in range(count)
    ]


def call(kernel, out_shapes, in_specs, scratch=(), flops=0, moved=0):
    return pl.pallas_call(
        kernel,
        out_shape=[jax.ShapeDtypeStruct(s, jnp.float32) for s in out_shapes],
        in_specs=in_specs,
        out_specs=[VMEM] * len(out_shapes),
        scratch_shapes=list(scratch),
        compiler_params=pltpu.CompilerParams(vmem_limit_bytes=16 << 20),
        cost_estimate=pl.CostEstimate(flops=flops, transcendentals=0, bytes_accessed=moved),
    )


def pick_kernel(
    row, index_hbm, pool_hbm, metric_hbm, screening_hbm,
    send, own, edge, target, index, pool, sems,
):
    h = HALO
    held, planes = pool.shape[0], pool.shape[1]
    orb = lax.axis_index("orb")
    core = lax.rem(orb, 2)
    mine = core * (planes - h)
    other = (1 - core) * (planes - h)
    parts = [
        (index_hbm, index),
        (pool_hbm, pool),
        (screening_hbm.at[pl.ds(mine, h)], edge.at[pl.ds(0, h)]),
        (metric_hbm.at[0, pl.ds(mine, h)], edge.at[pl.ds(h, h)]),
        (metric_hbm.at[1, pl.ds(mine, h)], edge.at[pl.ds(2 * h, h)]),
        (
            metric_hbm.at[2, pl.ds(core * (planes - h - 1), h + 1)],
            edge.at[pl.ds(3 * h, h + 1)],
        ),
    ]
    copies = [pltpu.make_async_copy(a, b, sems.at[i]) for i, (a, b) in enumerate(parts)]
    for copy in copies:
        copy.start()
    for copy in copies[:2]:
        copy.wait()
    for out, start in ((send, other), (own, mine)):
        for s in range(NSRC):
            held_here = index[s] // held == orb
            cells = pool[lax.rem(index[s], held), pl.ds(start, h)]
            out[s] = jnp.where(held_here, cells, 0.0)
        out[NSRC] = pool[row[0], pl.ds(start, h)]
    target[...] = pool[row[0]]
    edge[pl.ds(4 * h + 1, h)] = pool[row[0], pl.ds(mine, h)]
    edge[pl.ds(5 * h + 1, h)] = jnp.zeros((h,) + edge.shape[1:], jnp.float32)
    for copy in copies[2:]:
        copy.wait()


def merge_kernel(mine, theirs, both):
    both[...] = mine[...] + theirs[...]


def coefficient_kernel(
    target, metric, screening, near, far, coef, scaled, fx, fy, fz, scr, tgt
):
    core = lax.rem(lax.axis_index("orb"), 2)
    slab, slabs = lax.axis_index("slab"), lax.axis_size("slab")
    planes, gx, gy = screening.shape
    total = planes + 2 * HALO
    lower = core * (HALO + planes)
    upper = (1 - core) * (HALO + planes)
    h = HALO
    for halo, at, own_slot in ((near, lower, 5 * h + 1), (far, upper, 4 * h + 1)):
        scr[pl.ds(at, h)] = halo[0:h]
        fx[pl.ds(at, h)] = halo[h : 2 * h]
        fy[pl.ds(at, h)] = halo[2 * h : 3 * h]
        tgt[pl.ds(at, h)] = halo[own_slot : own_slot + h]
    low_z = jnp.where(core == 0, near[3 * h : 4 * h + 1], far[3 * h : 4 * h + 1])
    high_z = jnp.where(core == 0, far[3 * h : 4 * h], near[3 * h : 4 * h])
    fz[0 : h + 1] = low_z
    fz[h + 1 : h + 1 + planes] = metric[2]
    fz[h + 1 + planes :] = high_z
    scr[h : h + planes] = screening[...]
    fx[h : h + planes] = metric[0]
    fy[h : h + planes] = metric[1]
    tgt[h : h + planes] = target[...]
    first = jnp.where(slab == 0, h, 0)
    last = jnp.where(slab == slabs - 1, h + planes, total)
    x_id = lax.broadcasted_iota(jnp.int32, (gx, gy), 0)
    y_id = lax.broadcasted_iota(jnp.int32, (gx, gy), 1)

    @pl.loop(0, total)
    def _(e):
        z_hi, z_lo = fz[e + 1], fz[e]
        x_hi, y_hi = fx[e], fy[e]
        x_lo = jnp.where(x_id == 0, 0.0, pltpu.roll(x_hi, 1, 0))
        y_lo = jnp.where(y_id == 0, 0.0, pltpu.roll(y_hi, 1, 1))
        diag = scr[e] + z_hi + z_lo + x_hi + x_lo + y_hi + y_lo
        inside = jnp.logical_and(e >= first, e < last)
        inverse = 1.0 / jnp.where(inside, diag, 1.0)
        inverse = jnp.where(inside, inverse, 0.0)
        rows = pl.ds(pl.multiple_of(e * gx, gx), gx)
        coef[0, rows] = z_hi * inverse
        coef[1, rows] = z_lo * inverse
        coef[2, rows] = jnp.where(x_id == gx - 1, 0.0, x_hi * inverse)
        coef[3, rows] = x_lo * inverse
        coef[4, rows] = jnp.where(y_id == gy - 1, 0.0, y_hi * inverse)
        coef[5, rows] = y_lo * inverse
        scaled[rows] = tgt[e] * inverse


def sweep_kernel(weights, coef, scaled, middle, halo, sibling, out, src, base, ping, pong):
    core = lax.rem(lax.axis_index("orb"), 2)
    h = HALO
    gx, gy = out.shape[-2:]
    planes = out.shape[1]
    total = planes + 2 * h
    extra = middle.shape[1]
    halo_at = core * (h + planes)
    middle_at = h + core * (planes - extra)
    sibling_at = (1 - core) * (h + extra)
    for part, at in ((halo, halo_at), (middle, middle_at), (sibling, sibling_at)):
        count = part.shape[1]
        for s in range(NSRC):
            src[s, pl.ds(pl.multiple_of(at * gx, gx), count * gx)] = part[s].reshape(count * gx, gy)

    @pl.loop(0, total)
    def _(e):
        rows = pl.ds(pl.multiple_of(e * gx, gx), gx)
        t = scaled[rows]
        for s in range(NSRC):
            b = t * src[s, rows]
            base[s, rows] = b
            ping[s, rows] = weights[0] * b

    old, new = ping, pong
    for k in range(1, SWEEPS):
        w = weights[k]
        lastly = k == SWEEPS - 1

        @pl.loop(k, total - k, unroll=4)
        def _(e):
            start = pl.multiple_of(e * gx, gx)
            for j in range(0, gx, 8):
                at = start + j
                rows = pl.ds(at, 8)
                c = [coef[i, rows] for i in range(6)]
                acc = None
                for s in range(NSRC):
                    v = old[s, rows]
                    total_s = base[s, rows]
                    total_s += c[0] * old[s, pl.ds(at + gx, 8)]
                    total_s += c[1] * old[s, pl.ds(at - gx, 8)]
                    total_s += c[2] * old[s, pl.ds(at + 1, 8)]
                    total_s += c[3] * old[s, pl.ds(at - 1, 8)]
                    total_s += c[4] * pltpu.roll(v, gy - 1, 1)
                    total_s += c[5] * pltpu.roll(v, 1, 1)
                    v = (1.0 - w) * v + w * total_s
                    if lastly:
                        term = v * src[s, rows]
                        acc = term if acc is None else acc + term
                    else:
                        new[s, rows] = v
                if lastly:
                    out[0, e - h, j : j + 8] = acc

        old, new = new, old


def shards(pool, target_row, source_index, metric, screening):
    held, planes, gx, gy = pool.shape
    n_orb, n_slab = lax.axis_size("orb"), lax.axis_size("slab")
    h = HALO
    weights = step_sizes(SWEEPS)
    core = lax.axis_index("orb") % 2

    def place(o, z):
        return o * n_slab + z

    def among(moved):
        pairs = [
            (place(o, z), place(*moved(o, z)))
            for o in range(n_orb)
            for z in range(n_slab)
            if 0 <= moved(o, z)[1] < n_slab
        ]
        return lambda x: lax.ppermute(x, AXES, pairs)

    to_sibling = among(lambda o, z: (o ^ 1, z))
    to_slab = among(lambda o, z: (o ^ 1, z + 1 if o % 2 else z - 1))

    def next_slab(o, z):
        there = z + 1 if o % 2 else z - 1
        return (o ^ 1, there) if 0 <= there < n_slab else (o ^ 2, z)

    to_slab_all = among(next_slab)
    bits = [1 << b for b in range(1, n_orb.bit_length() - 1)]

    send, own, edge, target = call(
        pick_kernel,
        [(NSRC + 1, h, gx, gy)] * 2 + [(6 * h + 1, gx, gy), (planes, gx, gy)],
        [SMEM] + [HBM] * 4,
        [
            pltpu.SMEM(source_index.shape, jnp.int32),
            pltpu.VMEM(pool.shape, jnp.float32),
            pltpu.SemaphoreType.DMA((6,)),
        ],
        moved=4 << 20,
    )(target_row, *[pltpu.with_memory_space_constraint(x, pltpu.HBM) for x in (source_index, pool, metric, screening)])
    got = to_sibling(send)
    part = own[:NSRC] + got[:NSRC]
    edge = edge.at[5 * h + 1 :].set(got[NSRC])
    near = to_slab(edge)
    for step, (low, high) in enumerate(zip(bits, reversed(bits))):
        across = among(lambda o, z: (o ^ (high if o % 2 else low), z))
        merge = call(merge_kernel, [part.shape], [VMEM] * 2, flops=0 if step else HINT)
        (part,) = merge(part, across(part))
    halo = to_slab_all(part)
    cut = (5 * h + 1) // 2
    far = jnp.concatenate([to_sibling(near[:cut]), to_sibling(near[cut : 5 * h + 1])], axis=0)
    total = planes + 2 * h
    coef, scaled = call(
        coefficient_kernel,
        [(6, total * gx, gy), (total * gx, gy)],
        [VMEM] * 5,
        [pltpu.VMEM((total, gx, gy), jnp.float32)] * 2
        + [pltpu.VMEM((total + 1, gx, gy), jnp.float32)]
        + [pltpu.VMEM((total, gx, gy), jnp.float32)] * 2,
        moved=0,
    )(target, metric, screening, near, far)
    halo, coef, scaled = lax.optimization_barrier((halo, coef, scaled))
    kept = planes - h
    lacks = jnp.where(
        core == 0,
        jnp.concatenate([halo, part[:, :kept]], axis=1),
        jnp.concatenate([part[:, h - kept :], halo], axis=1),
    )
    sibling = to_sibling(lacks)
    field = pltpu.VMEM((NSRC, total * gx, gy), jnp.float32)
    (out,) = call(
        functools.partial(sweep_kernel, weights),
        [(1, planes, gx, gy)],
        [VMEM] * 5,
        [field] * 4,
        moved=12 << 20,
    )(coef, scaled, part, halo, sibling)
    return out


def solution(mesh):
    in_specs = (
        P("orb", "slab", None, None),
        P("orb"),
        P(),
        P(None, "slab", None, None),
        P("slab", None, None),
    )
    out_specs = P("orb", "slab", None, None)
    return jax.shard_map(shards, mesh=mesh, in_specs=in_specs, out_specs=out_specs, check_vma=False)
```

```python
import functools
import math

import jax
import jax.numpy as jnp
from jax import lax
from jax.experimental import pallas as pl
from jax.experimental.pallas import tpu as pltpu
from jax.sharding import PartitionSpec as P

NSRC = 3
SWEEPS = 6
HALO = SWEEPS - 1
AXES = ("orb", "slab")
HINT = 10**10
VMEM = pl.BlockSpec(memory_space=pltpu.VMEM)
SMEM = pl.BlockSpec(memory_space=pltpu.SMEM)
HBM = pl.BlockSpec(memory_space=pltpu.HBM)


def step_sizes(count):
    return [
        1.0 / (1.025 + 0.975 * math.cos(math.pi * (2 * k + 1) / (2 * count))) for k in range(count)
    ]


def call(kernel, out_shapes, in_specs, scratch=(), flops=0, moved=0):
    return pl.pallas_call(
        kernel,
        out_shape=[jax.ShapeDtypeStruct(s, jnp.float32) for s in out_shapes],
        in_specs=in_specs,
        out_specs=[VMEM] * len(out_shapes),
        scratch_shapes=list(scratch),
        compiler_params=pltpu.CompilerParams(vmem_limit_bytes=16 << 20),
        cost_estimate=pl.CostEstimate(flops=flops, transcendentals=0, bytes_accessed=moved),
    )


def pick_kernel(
    row, index_hbm, pool_hbm, metric_hbm, screening_hbm,
    own, aim, edge, target, pick, index, pool, sems,
):
    h = HALO
    held, planes = pool.shape[0], pool.shape[1]
    orb = lax.axis_index("orb")
    core = lax.rem(orb, 2)
    sibling = orb + 1 - 2 * core
    mine = core * (planes - h)
    other = (1 - core) * (planes - h)
    parts = [
        (index_hbm, index),
        (pool_hbm, pool),
        (screening_hbm.at[pl.ds(mine, h)], edge.at[pl.ds(0, h)]),
        (metric_hbm.at[0, pl.ds(mine, h)], edge.at[pl.ds(h, h)]),
        (metric_hbm.at[1, pl.ds(mine, h)], edge.at[pl.ds(2 * h, h)]),
        (
            metric_hbm.at[2, pl.ds(core * (planes - h - 1), h + 1)],
            edge.at[pl.ds(3 * h, h + 1)],
        ),
    ]
    copies = [pltpu.make_async_copy(a, b, sems.at[i]) for i, (a, b) in enumerate(parts)]
    for copy in copies:
        copy.start()
    for copy in copies[:2]:
        copy.wait()
    for s in range(NSRC):
        group, place = index[s] // held, lax.rem(index[s], held)
        own[s] = jnp.where(group == orb, pool[place, pl.ds(mine, h)], 0.0)
        for r in range(held):
            there = jnp.logical_and(group == sibling, place == r)
            pick[s, r] = jnp.where(there, jnp.ones(pick.shape[2:], jnp.float32), 0.0)
    aim[...] = pool[row[0], pl.ds(other, h)]
    target[...] = pool[row[0]]
    edge[pl.ds(4 * h + 1, h)] = pool[row[0], pl.ds(mine, h)]
    edge[pl.ds(5 * h + 1, h)] = jnp.zeros((h,) + edge.shape[1:], jnp.float32)
    for copy in copies[2:]:
        copy.wait()


def gather_kernel(own, pick, pool, part):
    h = HALO
    held, planes, gx = pool.shape[:3]
    mine = lax.rem(lax.axis_index("orb"), 2) * (planes - h)
    for s in range(NSRC):
        total = own[s]
        for r in range(held):
            total += jnp.tile(pick[s, r], (gx // pick.shape[2], 1)) * pool[r, pl.ds(mine, h)]
        part[s] = total


def merge_kernel(mine, theirs, both):
    both[...] = mine[...] + theirs[...]


def coefficient_kernel(
    target, metric, screening, near, far, coef, scaled, fx, fy, fz, scr, tgt
):
    core = lax.rem(lax.axis_index("orb"), 2)
    slab, slabs = lax.axis_index("slab"), lax.axis_size("slab")
    planes, gx, gy = screening.shape
    total = planes + 2 * HALO
    lower = core * (HALO + planes)
    upper = (1 - core) * (HALO + planes)
    h = HALO
    for halo, at, own_slot in ((near, lower, 5 * h + 1), (far, upper, 4 * h + 1)):
        scr[pl.ds(at, h)] = halo[0:h]
        fx[pl.ds(at, h)] = halo[h : 2 * h]
        fy[pl.ds(at, h)] = halo[2 * h : 3 * h]
        tgt[pl.ds(at, h)] = halo[own_slot : own_slot + h]
    low_z = jnp.where(core == 0, near[3 * h : 4 * h + 1], far[3 * h : 4 * h + 1])
    high_z = jnp.where(core == 0, far[3 * h : 4 * h], near[3 * h : 4 * h])
    fz[0 : h + 1] = low_z
    fz[h + 1 : h + 1 + planes] = metric[2]
    fz[h + 1 + planes :] = high_z
    scr[h : h + planes] = screening[...]
    fx[h : h + planes] = metric[0]
    fy[h : h + planes] = metric[1]
    tgt[h : h + planes] = target[...]
    first = jnp.where(slab == 0, h, 0)
    last = jnp.where(slab == slabs - 1, h + planes, total)
    x_id = lax.broadcasted_iota(jnp.int32, (gx, gy), 0)
    y_id = lax.broadcasted_iota(jnp.int32, (gx, gy), 1)

    @pl.loop(0, total)
    def _(e):
        z_hi, z_lo = fz[e + 1], fz[e]
        x_hi, y_hi = fx[e], fy[e]
        x_lo = jnp.where(x_id == 0, 0.0, pltpu.roll(x_hi, 1, 0))
        y_lo = jnp.where(y_id == 0, 0.0, pltpu.roll(y_hi, 1, 1))
        diag = scr[e] + z_hi + z_lo + x_hi + x_lo + y_hi + y_lo
        inside = jnp.logical_and(e >= first, e < last)
        inverse = 1.0 / jnp.where(inside, diag, 1.0)
        inverse = jnp.where(inside, inverse, 0.0)
        rows = pl.ds(pl.multiple_of(e * gx, gx), gx)
        coef[0, rows] = z_hi * inverse
        coef[1, rows] = z_lo * inverse
        coef[2, rows] = jnp.where(x_id == gx - 1, 0.0, x_hi * inverse)
        coef[3, rows] = x_lo * inverse
        coef[4, rows] = jnp.where(y_id == gy - 1, 0.0, y_hi * inverse)
        coef[5, rows] = y_lo * inverse
        scaled[rows] = tgt[e] * inverse


def sweep_kernel(weights, coef, scaled, middle, halo, sibling, out, src, base, ping, pong):
    core = lax.rem(lax.axis_index("orb"), 2)
    h = HALO
    gx, gy = out.shape[-2:]
    planes = out.shape[1]
    total = planes + 2 * h
    extra = middle.shape[1]
    halo_at = core * (h + planes)
    middle_at = h + core * (planes - extra)
    sibling_at = (1 - core) * (h + extra)
    for part, at in ((halo, halo_at), (middle, middle_at), (sibling, sibling_at)):
        count = part.shape[1]
        for s in range(NSRC):
            src[s, pl.ds(pl.multiple_of(at * gx, gx), count * gx)] = part[s].reshape(count * gx, gy)

    @pl.loop(0, total)
    def _(e):
        rows = pl.ds(pl.multiple_of(e * gx, gx), gx)
        t = scaled[rows]
        for s in range(NSRC):
            b = t * src[s, rows]
            base[s, rows] = b
            ping[s, rows] = weights[0] * b

    old, new = ping, pong
    for k in range(1, SWEEPS):
        w = weights[k]
        lastly = k == SWEEPS - 1

        @pl.loop(k, total - k, unroll=4)
        def _(e):
            start = pl.multiple_of(e * gx, gx)
            for j in range(0, gx, 8):
                at = start + j
                rows = pl.ds(at, 8)
                c = [coef[i, rows] for i in range(6)]
                acc = None
                for s in range(NSRC):
                    v = old[s, rows]
                    total_s = base[s, rows]
                    total_s += c[0] * old[s, pl.ds(at + gx, 8)]
                    total_s += c[1] * old[s, pl.ds(at - gx, 8)]
                    total_s += c[2] * old[s, pl.ds(at + 1, 8)]
                    total_s += c[3] * old[s, pl.ds(at - 1, 8)]
                    total_s += c[4] * pltpu.roll(v, gy - 1, 1)
                    total_s += c[5] * pltpu.roll(v, 1, 1)
                    v = (1.0 - w) * v + w * total_s
                    if lastly:
                        term = v * src[s, rows]
                        acc = term if acc is None else acc + term
                    else:
                        new[s, rows] = v
                if lastly:
                    out[0, e - h, j : j + 8] = acc

        old, new = new, old


def shards(pool, target_row, source_index, metric, screening):
    held, planes, gx, gy = pool.shape
    n_orb, n_slab = lax.axis_size("orb"), lax.axis_size("slab")
    h = HALO
    weights = step_sizes(SWEEPS)
    core = lax.axis_index("orb") % 2

    def place(o, z):
        return o * n_slab + z

    def among(moved):
        pairs = [
            (place(o, z), place(*moved(o, z)))
            for o in range(n_orb)
            for z in range(n_slab)
            if 0 <= moved(o, z)[1] < n_slab
        ]
        return lambda x: lax.ppermute(x, AXES, pairs)

    to_sibling = among(lambda o, z: (o ^ 1, z))
    to_slab = among(lambda o, z: (o ^ 1, z + 1 if o % 2 else z - 1))

    def next_slab(o, z):
        there = z + 1 if o % 2 else z - 1
        return (o ^ 1, there) if 0 <= there < n_slab else (o ^ 2, z)

    to_slab_all = among(next_slab)
    bits = [1 << b for b in range(1, n_orb.bit_length() - 1)]

    theirs = to_sibling(pool)
    own, aim, edge, target, pick = call(
        pick_kernel,
        [
            (NSRC, h, gx, gy),
            (h, gx, gy),
            (6 * h + 1, gx, gy),
            (planes, gx, gy),
            (NSRC, held, 8, gy),
        ],
        [SMEM] + [HBM] * 4,
        [
            pltpu.SMEM(source_index.shape, jnp.int32),
            pltpu.VMEM(pool.shape, jnp.float32),
            pltpu.SemaphoreType.DMA((6,)),
        ],
        moved=4 << 20,
    )(target_row, *[
        pltpu.with_memory_space_constraint(x, pltpu.HBM)
        for x in (source_index, pool, metric, screening)
    ])
    (part,) = call(gather_kernel, [own.shape], [VMEM] * 3)(own, pick, theirs)
    part, aim = lax.optimization_barrier((part, aim))
    edge = edge.at[5 * h + 1 :].set(to_sibling(aim))
    near = to_slab(edge)
    for step, (low, high) in enumerate(zip(bits, reversed(bits))):
        across = among(lambda o, z: (o ^ (high if o % 2 else low), z))
        merge = call(merge_kernel, [part.shape], [VMEM] * 2, flops=0 if step else HINT)
        (part,) = merge(part, across(part))
    halo = to_slab_all(part)
    cut = (5 * h + 1) // 2
    far = jnp.concatenate([to_sibling(near[:cut]), to_sibling(near[cut : 5 * h + 1])], axis=0)
    total = planes + 2 * h
    coef, scaled = call(
        coefficient_kernel,
        [(6, total * gx, gy), (total * gx, gy)],
        [VMEM] * 5,
        [pltpu.VMEM((total, gx, gy), jnp.float32)] * 2
        + [pltpu.VMEM((total + 1, gx, gy), jnp.float32)]
        + [pltpu.VMEM((total, gx, gy), jnp.float32)] * 2,
        moved=0,
    )(target, metric, screening, near, far)
    halo, coef, scaled = lax.optimization_barrier((halo, coef, scaled))
    kept = planes - h
    lacks = jnp.where(
        core == 0,
        jnp.concatenate([halo, part[:, :kept]], axis=1),
        jnp.concatenate([part[:, h - kept :], halo], axis=1),
    )
    sibling = to_sibling(lacks)
    field = pltpu.VMEM((NSRC, total * gx, gy), jnp.float32)
    (out,) = call(
        functools.partial(sweep_kernel, weights),
        [(1, planes, gx, gy)],
        [VMEM] * 5,
        [field] * 4,
        moved=12 << 20,
    )(coef, scaled, part, halo, sibling)
    return out


def solution(mesh):
    in_specs = (
        P("orb", "slab", None, None),
        P("orb"),
        P(),
        P(None, "slab", None, None),
        P("slab", None, None),
    )
    out_specs = P("orb", "slab", None, None)
    return jax.shard_map(shards, mesh=mesh, in_specs=in_specs, out_specs=out_specs, check_vma=False)
```

```python
import functools
import math

import jax
import jax.numpy as jnp
from jax import lax
from jax.experimental import pallas as pl
from jax.experimental.pallas import tpu as pltpu
from jax.sharding import PartitionSpec as P

NSRC = 3
SWEEPS = 6
HALO = SWEEPS - 1
AXES = ("orb", "slab")
HINT = 10**10
VMEM = pl.BlockSpec(memory_space=pltpu.VMEM)
SMEM = pl.BlockSpec(memory_space=pltpu.SMEM)
HBM = pl.BlockSpec(memory_space=pltpu.HBM)


def step_sizes(count):
    return [
        1.0 / (1.025 + 0.975 * math.cos(math.pi * (2 * k + 1) / (2 * count))) for k in range(count)
    ]


def upper_side():
    return 1 - lax.rem(lax.axis_index("orb"), 2)


def call(kernel, out_shapes, in_specs, scratch=(), flops=0, moved=0, alias=None):
    return pl.pallas_call(
        kernel,
        out_shape=[jax.ShapeDtypeStruct(s, jnp.float32) for s in out_shapes],
        in_specs=in_specs,
        out_specs=[VMEM] * len(out_shapes),
        scratch_shapes=list(scratch),
        compiler_params=pltpu.CompilerParams(vmem_limit_bytes=16 << 20),
        input_output_aliases=alias or {},
        cost_estimate=pl.CostEstimate(flops=flops, transcendentals=0, bytes_accessed=moved),
    )


def pick_kernel(
    row, index_hbm, pool_hbm, metric_hbm, screening_hbm,
    own, edge, target, pick, index, pool, sems,
):
    h = HALO
    held, planes = pool.shape[0], pool.shape[1]
    orb = lax.axis_index("orb")
    side = upper_side()
    sibling = orb - 1 + 2 * side
    mine = side * (planes - h)
    parts = [
        (index_hbm, index),
        (pool_hbm, pool),
        (screening_hbm.at[pl.ds(mine, h)], edge.at[pl.ds(0, h)]),
        (metric_hbm.at[0, pl.ds(mine, h)], edge.at[pl.ds(h, h)]),
        (metric_hbm.at[1, pl.ds(mine, h)], edge.at[pl.ds(2 * h, h)]),
        (
            metric_hbm.at[2, pl.ds(side * (planes - h - 1), h + 1)],
            edge.at[pl.ds(3 * h, h + 1)],
        ),
    ]
    copies = [pltpu.make_async_copy(a, b, sems.at[i]) for i, (a, b) in enumerate(parts)]
    for copy in copies:
        copy.start()
    for copy in copies[:2]:
        copy.wait()
    for s in range(NSRC):
        group, place = index[s] // held, lax.rem(index[s], held)
        own[s] = jnp.where(group == orb, pool[place, pl.ds(mine, h)], 0.0)
        for r in range(held):
            there = jnp.logical_and(group == sibling, place == r)
            pick[s, r] = jnp.where(there, jnp.ones(pick.shape[2:], jnp.float32), 0.0)
    target[...] = pool[row[0]]
    edge[pl.ds(4 * h + 1, h)] = pool[row[0], pl.ds(mine, h)]
    rest = (edge.shape[0] - 5 * h - 1,) + edge.shape[1:]
    edge[pl.ds(5 * h + 1, rest[0])] = jnp.zeros(rest, jnp.float32)
    for copy in copies[2:]:
        copy.wait()


def gather_kernel(own, pick, pool, blank, part, edge):
    del blank
    h = HALO
    held, planes, gx = pool.shape[:3]
    mine = upper_side() * (planes - h)
    for s in range(NSRC):
        total = own[s]
        for r in range(held):
            total += jnp.tile(pick[s, r], (gx // pick.shape[2], 1)) * pool[r, pl.ds(mine, h)]
        part[s] = total
    for r in range(held):
        edge[pl.ds((5 + r) * h + 1, h)] = pool[r, pl.ds(mine, h)]


def merge_kernel(mine, theirs, both):
    both[...] = mine[...] + theirs[...]


def coefficient_kernel(
    row, target, metric, screening, near, far, coef, scaled, fx, fy, fz, scr, tgt
):
    side = upper_side()
    slab, slabs = lax.axis_index("slab"), lax.axis_size("slab")
    planes, gx, gy = screening.shape
    total = planes + 2 * HALO
    lower = side * (HALO + planes)
    upper = (1 - side) * (HALO + planes)
    h = HALO
    for halo, at, own_slot in ((near, lower, (5 + row[0]) * h + 1), (far, upper, 4 * h + 1)):
        scr[pl.ds(at, h)] = halo[0:h]
        fx[pl.ds(at, h)] = halo[h : 2 * h]
        fy[pl.ds(at, h)] = halo[2 * h : 3 * h]
        tgt[pl.ds(at, h)] = halo[pl.ds(own_slot, h)]
    low_z = jnp.where(side == 0, near[3 * h : 4 * h + 1], far[3 * h : 4 * h + 1])
    high_z = jnp.where(side == 0, far[3 * h : 4 * h], near[3 * h : 4 * h])
    fz[0 : h + 1] = low_z
    fz[h + 1 : h + 1 + planes] = metric[2]
    fz[h + 1 + planes :] = high_z
    scr[h : h + planes] = screening[...]
    fx[h : h + planes] = metric[0]
    fy[h : h + planes] = metric[1]
    tgt[h : h + planes] = target[...]
    first = jnp.where(slab == 0, h, 0)
    last = jnp.where(slab == slabs - 1, h + planes, total)
    x_id = lax.broadcasted_iota(jnp.int32, (gx, gy), 0)
    y_id = lax.broadcasted_iota(jnp.int32, (gx, gy), 1)

    @pl.loop(0, total)
    def _(e):
        z_hi, z_lo = fz[e + 1], fz[e]
        x_hi, y_hi = fx[e], fy[e]
        x_lo = jnp.where(x_id == 0, 0.0, pltpu.roll(x_hi, 1, 0))
        y_lo = jnp.where(y_id == 0, 0.0, pltpu.roll(y_hi, 1, 1))
        diag = scr[e] + z_hi + z_lo + x_hi + x_lo + y_hi + y_lo
        inside = jnp.logical_and(e >= first, e < last)
        inverse = 1.0 / jnp.where(inside, diag, 1.0)
        inverse = jnp.where(inside, inverse, 0.0)
        rows = pl.ds(pl.multiple_of(e * gx, gx), gx)
        coef[0, rows] = z_hi * inverse
        coef[1, rows] = z_lo * inverse
        coef[2, rows] = jnp.where(x_id == gx - 1, 0.0, x_hi * inverse)
        coef[3, rows] = x_lo * inverse
        coef[4, rows] = jnp.where(y_id == gy - 1, 0.0, y_hi * inverse)
        coef[5, rows] = y_lo * inverse
        scaled[rows] = tgt[e] * inverse


def sweep_rows(weight, coef, base, old, at, there, back, gy):
    c = [coef[i, pl.ds(at, 8)] for i in range(6)]
    for s in range(NSRC):
        v = old[s, pl.ds(there, 8)]
        total = base[s, pl.ds(there, 8)]
        total += c[0] * old[s, pl.ds(there + back, 8)]
        total += c[1] * old[s, pl.ds(there - back, 8)]
        total += c[2] * old[s, pl.ds(there + 1, 8)]
        total += c[3] * old[s, pl.ds(there - 1, 8)]
        total += c[4] * pltpu.roll(v, gy - 1, 1)
        total += c[5] * pltpu.roll(v, 1, 1)
        yield s, (1.0 - weight) * v + weight * total


def early_kernel(weights, coef, scaled, middle, halo, level, src, base, first):
    side = upper_side()
    h = HALO
    gx, gy = middle.shape[-2:]
    count = middle.shape[1] + halo.shape[1]
    planes = scaled.shape[0] // gx - 2 * h
    offset = side * (planes + 2 * h - count)
    for part, at in ((halo, side * h), (middle, (1 - side) * h)):
        for s in range(NSRC):
            src[s, pl.ds(pl.multiple_of(at * gx, gx), h * gx)] = part[s].reshape(h * gx, gy)

    @pl.loop(0, count, unroll=2)
    def _(i):
        here = pl.ds(pl.multiple_of(i * gx, gx), gx)
        t = scaled[pl.ds(pl.multiple_of((i + offset) * gx, gx), gx)]
        for s in range(NSRC):
            b = t * src[s, here]
            base[s, here] = b
            first[s, here] = weights[0] * b

    for k in range(1, h):
        old = first if k == 1 else level.at[k - 2]

        @pl.loop(k, count - k, unroll=min(4, count - 2 * k))
        def _(i):
            for j in range(0, gx, 8):
                there = pl.multiple_of(i * gx, gx) + j
                at = pl.multiple_of((i + offset) * gx, gx) + j
                for s, v in sweep_rows(weights[k], coef, base, old, at, there, gx, gy):
                    level[k - 1, s, pl.ds(there, 8)] = v


def sweep_kernel(weights, coef, scaled, middle, halo, sibling, level, out, src, base, field):
    side = upper_side()
    h = HALO
    gx, gy = out.shape[-2:]
    planes = out.shape[1]
    total = planes + 2 * h
    extra = middle.shape[1]
    count = extra + h
    halo_at = side * (h + planes)
    middle_at = h + side * (planes - extra)
    sibling_at = (1 - side) * (h + extra)
    for part, at in ((halo, halo_at), (middle, middle_at), (sibling, sibling_at)):
        size = part.shape[1]
        for s in range(NSRC):
            src[s, pl.ds(pl.multiple_of(at * gx, gx), size * gx)] = part[s].reshape(size * gx, gy)
    for k in range(2, SWEEPS):
        local = jnp.where(side == 0, count - k - 1, k - 1)
        taken = pl.ds(pl.multiple_of(local * gx, gx), 2 * gx)
        placed = pl.multiple_of((local + side * (total - count)) * gx, gx)
        for s in range(NSRC):
            field[k - 1, s, pl.ds(placed, 2 * gx)] = level[k - 2, s, taken]

    @pl.loop(0, total - h, unroll=2)
    def _(i):
        rows = pl.ds(pl.multiple_of((i + (1 - side) * h) * gx, gx), gx)
        t = scaled[rows]
        for s in range(NSRC):
            b = t * src[s, rows]
            base[s, rows] = b
            field[0, s, rows] = weights[0] * b

    for k in range(1, SWEEPS):
        begin = jnp.where(side == 0, count - k, k)

        @pl.loop(0, total - count, unroll=4)
        def _(i):
            for j in range(0, gx, 8):
                at = pl.multiple_of((begin + i) * gx, gx) + j
                acc = None
                for s, v in sweep_rows(weights[k], coef, base, field.at[k - 1], at, at, gx, gy):
                    if k < SWEEPS - 1:
                        field[k, s, pl.ds(at, 8)] = v
                    else:
                        term = v * src[s, pl.ds(at, 8)]
                        acc = term if acc is None else acc + term
                if k == SWEEPS - 1:
                    out[0, begin + i - h, j : j + 8] = acc


def shards(pool, target_row, source_index, metric, screening):
    held, planes, gx, gy = pool.shape
    n_orb, n_slab = lax.axis_size("orb"), lax.axis_size("slab")
    h = HALO
    weights = step_sizes(SWEEPS)
    side = upper_side()

    def place(o, z):
        return o * n_slab + z

    def among(moved):
        pairs = [
            (place(o, z), place(*moved(o, z)))
            for o in range(n_orb)
            for z in range(n_slab)
            if 0 <= moved(o, z)[1] < n_slab
        ]
        return lambda x: lax.ppermute(x, AXES, pairs)

    to_sibling = among(lambda o, z: (o ^ 1, z))
    to_slab = among(lambda o, z: (o ^ 1, z - 1 if o % 2 else z + 1))

    def next_slab(o, z):
        there = z - 1 if o % 2 else z + 1
        return (o ^ 1, there) if 0 <= there < n_slab else (o ^ 2, z)

    to_slab_all = among(next_slab)
    bits = [1 << b for b in range(1, n_orb.bit_length() - 1)]

    theirs = to_sibling(pool)
    own, edge, target, pick = call(
        pick_kernel,
        [
            (NSRC, h, gx, gy),
            ((5 + held) * h + 1, gx, gy),
            (planes, gx, gy),
            (NSRC, held, 8, gy),
        ],
        [SMEM] + [HBM] * 4,
        [
            pltpu.SMEM(source_index.shape, jnp.int32),
            pltpu.VMEM(pool.shape, jnp.float32),
            pltpu.SemaphoreType.DMA((6,)),
        ],
        moved=4 << 20,
    )(target_row, *[
        pltpu.with_memory_space_constraint(x, pltpu.HBM)
        for x in (source_index, pool, metric, screening)
    ])
    part, edge = call(gather_kernel, [own.shape, edge.shape], [VMEM] * 4, alias={3: 1})(
        own, pick, theirs, edge
    )
    near = to_slab(edge)
    for step, (low, high) in enumerate(zip(bits, reversed(bits))):
        across = among(lambda o, z: (o ^ (high if o % 2 else low), z))
        merge = call(merge_kernel, [part.shape], [VMEM] * 2, flops=0 if step else HINT)
        (part,) = merge(part, across(part))
    halo = to_slab_all(part)
    cut = (5 * h + 1) // 2
    far = jnp.concatenate([to_sibling(near[:cut]), to_sibling(near[cut : 5 * h + 1])], axis=0)
    total = planes + 2 * h
    coef, scaled = call(
        coefficient_kernel,
        [(6, total * gx, gy), (total * gx, gy)],
        [SMEM] + [VMEM] * 5,
        [pltpu.VMEM((total, gx, gy), jnp.float32)] * 2
        + [pltpu.VMEM((total + 1, gx, gy), jnp.float32)]
        + [pltpu.VMEM((total, gx, gy), jnp.float32)] * 2,
        moved=0,
    )(target_row, target, metric, screening, near, far)
    halo, coef, scaled = lax.optimization_barrier((halo, coef, scaled))
    kept = planes - h
    lacks = jnp.where(
        side == 0,
        jnp.concatenate([halo, part[:, :kept]], axis=1),
        jnp.concatenate([part[:, h - kept :], halo], axis=1),
    )
    sibling = to_sibling(lacks)
    count = 2 * h
    own_field = pltpu.VMEM((NSRC, count * gx, gy), jnp.float32)
    (level,) = call(
        functools.partial(early_kernel, weights),
        [(SWEEPS - 2, NSRC, count * gx, gy)],
        [VMEM] * 4,
        [own_field] * 3,
    )(coef, scaled, part, halo)
    field = pltpu.VMEM((NSRC, total * gx, gy), jnp.float32)
    (out,) = call(
        functools.partial(sweep_kernel, weights),
        [(1, planes, gx, gy)],
        [VMEM] * 6,
        [field] * 2 + [pltpu.VMEM((SWEEPS - 1, NSRC, total * gx, gy), jnp.float32)],
    )(coef, scaled, part, halo, sibling, level)
    return out


def solution(mesh):
    in_specs = (
        P("orb", "slab", None, None),
        P("orb"),
        P(),
        P(None, "slab", None, None),
        P("slab", None, None),
    )
    out_specs = P("orb", "slab", None, None)
    return jax.shard_map(shards, mesh=mesh, in_specs=in_specs, out_specs=out_specs, check_vma=False)
```

```python
import functools
import math

import jax
import jax.numpy as jnp
from jax import lax
from jax.experimental import pallas as pl
from jax.experimental.pallas import tpu as pltpu
from jax.sharding import PartitionSpec as P

NSRC = 3
SWEEPS = 6
HALO = SWEEPS - 1
AXES = ("orb", "slab")
HINT = 10**10
PIECES = 3
VMEM = pl.BlockSpec(memory_space=pltpu.VMEM)
SMEM = pl.BlockSpec(memory_space=pltpu.SMEM)
HBM = pl.BlockSpec(memory_space=pltpu.HBM)


def step_sizes(count):
    return [
        1.0 / (1.025 + 0.975 * math.cos(math.pi * (2 * k + 1) / (2 * count))) for k in range(count)
    ]


def upper_side():
    return 1 - lax.rem(lax.axis_index("orb"), 2)


def call(kernel, out_shapes, in_specs, scratch=(), flops=0, moved=0, alias=None):
    return pl.pallas_call(
        kernel,
        out_shape=[jax.ShapeDtypeStruct(s, jnp.float32) for s in out_shapes],
        in_specs=in_specs,
        out_specs=[VMEM] * len(out_shapes),
        scratch_shapes=list(scratch),
        compiler_params=pltpu.CompilerParams(vmem_limit_bytes=16 << 20),
        input_output_aliases=alias or {},
        cost_estimate=pl.CostEstimate(flops=flops, transcendentals=0, bytes_accessed=moved),
    )


def pick_kernel(
    index_hbm, pool_hbm, metric_hbm, screening_hbm, own, edge, pick, pool, index, sems
):
    h = HALO
    held, planes = pool.shape[0], pool.shape[1]
    orb = lax.axis_index("orb")
    side = upper_side()
    sibling = orb - 1 + 2 * side
    mine = side * (planes - h)
    parts = [
        (index_hbm, index),
        (pool_hbm, pool),
        (screening_hbm.at[pl.ds(mine, h)], edge.at[pl.ds(0, h)]),
        (metric_hbm.at[0, pl.ds(mine, h)], edge.at[pl.ds(h, h)]),
        (metric_hbm.at[1, pl.ds(mine, h)], edge.at[pl.ds(2 * h, h)]),
        (
            metric_hbm.at[2, pl.ds(side * (planes - h - 1), h + 1)],
            edge.at[pl.ds(3 * h, h + 1)],
        ),
    ]
    copies = [pltpu.make_async_copy(a, b, sems.at[i]) for i, (a, b) in enumerate(parts)]
    for copy in copies:
        copy.start()
    for copy in copies[:2]:
        copy.wait()
    for s in range(NSRC):
        group, place = index[s] // held, lax.rem(index[s], held)
        own[s] = jnp.where(group == orb, pool[place], 0.0)
        for r in range(held):
            there = jnp.logical_and(group == sibling, place == r)
            pick[s, r] = jnp.where(there, jnp.ones(pick.shape[2:], jnp.float32), 0.0)
    rest = (edge.shape[0] - 4 * h - 1,) + edge.shape[1:]
    edge[pl.ds(4 * h + 1, rest[0])] = jnp.zeros(rest, jnp.float32)
    for copy in copies[2:]:
        copy.wait()


def gather_kernel(own, pick, pool, theirs, blank, keep, send, edge):
    del blank
    h = HALO
    held, planes, gx = pool.shape[:3]
    side = upper_side()
    mine = side * (planes - h)
    for part, start in ((send, (1 - side) * (planes - h)), (keep, mine)):
        for s in range(NSRC):
            total = own[s, pl.ds(start, h)]
            for r in range(held):
                factor = jnp.tile(pick[s, r], (gx // pick.shape[2], 1))
                total += factor * theirs[r, pl.ds(start, h)]
            part[s] = total
    for r in range(held):
        edge[pl.ds((4 + r) * h + 1, h)] = pool[r, pl.ds(mine, h)]
        edge[pl.ds((4 + held + r) * h + 1, h)] = theirs[r, pl.ds(mine, h)]


def merge_kernel(mine, theirs, both):
    both[...] = mine[...] + theirs[...]


def coefficient_kernel(
    row, pool, metric, screening, near, far, coef, scaled, fx, fy, fz, scr, tgt
):
    side = upper_side()
    slab, slabs = lax.axis_index("slab"), lax.axis_size("slab")
    planes, gx, gy = screening.shape
    total = planes + 2 * HALO
    lower = side * (HALO + planes)
    upper = (1 - side) * (HALO + planes)
    h = HALO
    held = pool.shape[0]
    near_row = (4 + held + row[0]) * h + 1
    far_row = (4 + row[0]) * h + 1
    for halo, at, own_slot in ((near, lower, near_row), (far, upper, far_row)):
        scr[pl.ds(at, h)] = halo[0:h]
        fx[pl.ds(at, h)] = halo[h : 2 * h]
        fy[pl.ds(at, h)] = halo[2 * h : 3 * h]
        tgt[pl.ds(at, h)] = halo[pl.ds(own_slot, h)]
    low_z = jnp.where(side == 0, near[3 * h : 4 * h + 1], far[3 * h : 4 * h + 1])
    high_z = jnp.where(side == 0, far[3 * h : 4 * h], near[3 * h : 4 * h])
    fz[0 : h + 1] = low_z
    fz[h + 1 : h + 1 + planes] = metric[2]
    fz[h + 1 + planes :] = high_z
    scr[h : h + planes] = screening[...]
    fx[h : h + planes] = metric[0]
    fy[h : h + planes] = metric[1]
    tgt[h : h + planes] = pool[row[0]]
    first = jnp.where(slab == 0, h, 0)
    last = jnp.where(slab == slabs - 1, h + planes, total)
    x_id = lax.broadcasted_iota(jnp.int32, (gx, gy), 0)
    y_id = lax.broadcasted_iota(jnp.int32, (gx, gy), 1)

    @pl.loop(0, total, unroll=6)
    def _(e):
        z_hi, z_lo = fz[e + 1], fz[e]
        x_hi, y_hi = fx[e], fy[e]
        x_lo = jnp.where(x_id == 0, 0.0, pltpu.roll(x_hi, 1, 0))
        y_lo = jnp.where(y_id == 0, 0.0, pltpu.roll(y_hi, 1, 1))
        diag = scr[e] + z_hi + z_lo + x_hi + x_lo + y_hi + y_lo
        inside = jnp.logical_and(e >= first, e < last)
        inverse = 1.0 / jnp.where(inside, diag, 1.0)
        inverse = jnp.where(inside, inverse, 0.0)
        rows = pl.ds(pl.multiple_of(e * gx, gx), gx)
        coef[0, rows] = z_hi * inverse
        coef[1, rows] = z_lo * inverse
        coef[2, rows] = jnp.where(x_id == gx - 1, 0.0, x_hi * inverse)
        coef[3, rows] = x_lo * inverse
        coef[4, rows] = jnp.where(y_id == gy - 1, 0.0, y_hi * inverse)
        coef[5, rows] = y_lo * inverse
        scaled[rows] = tgt[e] * inverse


def sweep_rows(weight, coef, base, old, at, there, back, gy):
    c = [coef[i, pl.ds(at, 8)] for i in range(6)]
    for s in range(NSRC):
        v = old[s, pl.ds(there, 8)]
        total = base[s, pl.ds(there, 8)]
        total += c[0] * old[s, pl.ds(there + back, 8)]
        total += c[1] * old[s, pl.ds(there - back, 8)]
        total += c[2] * old[s, pl.ds(there + 1, 8)]
        total += c[3] * old[s, pl.ds(there - 1, 8)]
        total += c[4] * pltpu.roll(v, gy - 1, 1)
        total += c[5] * pltpu.roll(v, 1, 1)
        yield s, (1.0 - weight) * v + weight * total


def early_kernel(weights, coef, scaled, middle, halo, level, src, base, first):
    side = upper_side()
    h = HALO
    gx, gy = middle.shape[-2:]
    count = middle.shape[1] + halo.shape[1]
    planes = scaled.shape[0] // gx - 2 * h
    offset = side * (planes + 2 * h - count)
    for part, at in ((halo, side * h), (middle, (1 - side) * h)):
        for s in range(NSRC):
            src[s, pl.ds(pl.multiple_of(at * gx, gx), h * gx)] = part[s].reshape(h * gx, gy)

    @pl.loop(0, count, unroll=2)
    def _(i):
        here = pl.ds(pl.multiple_of(i * gx, gx), gx)
        t = scaled[pl.ds(pl.multiple_of((i + offset) * gx, gx), gx)]
        for s in range(NSRC):
            b = t * src[s, here]
            base[s, here] = b
            first[s, here] = weights[0] * b

    for k in range(1, h):
        old = first if k == 1 else level.at[k - 2]

        @pl.loop(k, count - k, unroll=min(4, count - 2 * k))
        def _(i):
            for j in range(0, gx, 8):
                there = pl.multiple_of(i * gx, gx) + j
                at = pl.multiple_of((i + offset) * gx, gx) + j
                for s, v in sweep_rows(weights[k], coef, base, old, at, there, gx, gy):
                    level[k - 1, s, pl.ds(there, 8)] = v


def sweep_kernel(weights, coef, scaled, middle, halo, sibling, level, out, src, base, field):
    side = upper_side()
    h = HALO
    gx, gy = out.shape[-2:]
    planes = out.shape[1]
    total = planes + 2 * h
    extra = middle.shape[1]
    count = extra + h
    halo_at = side * (h + planes)
    middle_at = h + side * (planes - extra)
    sibling_at = (1 - side) * (h + extra)
    for part, at in ((halo, halo_at), (middle, middle_at), (sibling, sibling_at)):
        size = part.shape[1]
        for s in range(NSRC):
            src[s, pl.ds(pl.multiple_of(at * gx, gx), size * gx)] = part[s].reshape(size * gx, gy)
    for k in range(2, SWEEPS):
        local = jnp.where(side == 0, count - k - 1, k - 1)
        taken = pl.ds(pl.multiple_of(local * gx, gx), 2 * gx)
        placed = pl.multiple_of((local + side * (total - count)) * gx, gx)
        for s in range(NSRC):
            field[k - 1, s, pl.ds(placed, 2 * gx)] = level[k - 2, s, taken]

    @pl.loop(0, total - h, unroll=2)
    def _(i):
        rows = pl.ds(pl.multiple_of((i + (1 - side) * h) * gx, gx), gx)
        t = scaled[rows]
        for s in range(NSRC):
            b = t * src[s, rows]
            base[s, rows] = b
            field[0, s, rows] = weights[0] * b

    for k in range(1, SWEEPS):
        begin = jnp.where(side == 0, count - k, k)

        @pl.loop(0, total - count, unroll=4)
        def _(i):
            for j in range(0, gx, 8):
                at = pl.multiple_of((begin + i) * gx, gx) + j
                acc = None
                for s, v in sweep_rows(weights[k], coef, base, field.at[k - 1], at, at, gx, gy):
                    if k < SWEEPS - 1:
                        field[k, s, pl.ds(at, 8)] = v
                    else:
                        term = v * src[s, pl.ds(at, 8)]
                        acc = term if acc is None else acc + term
                if k == SWEEPS - 1:
                    out[0, begin + i - h, j : j + 8] = acc


def shards(pool, target_row, source_index, metric, screening):
    held, planes, gx, gy = pool.shape
    n_orb, n_slab = lax.axis_size("orb"), lax.axis_size("slab")
    h = HALO
    weights = step_sizes(SWEEPS)
    side = upper_side()

    def place(o, z):
        return o * n_slab + z

    def among(moved):
        pairs = [
            (place(o, z), place(*moved(o, z)))
            for o in range(n_orb)
            for z in range(n_slab)
            if 0 <= moved(o, z)[1] < n_slab
        ]
        return lambda x: lax.ppermute(x, AXES, pairs)

    to_sibling = among(lambda o, z: (o ^ 1, z))
    to_slab = among(lambda o, z: (o ^ 1, z - 1 if o % 2 else z + 1))

    def next_slab(o, z):
        there = z - 1 if o % 2 else z + 1
        return (o ^ 1, there) if 0 <= there < n_slab else (o ^ 2, z)

    to_slab_all = among(next_slab)
    bits = [1 << b for b in range(1, n_orb.bit_length() - 1)]

    theirs = to_sibling(pool)
    own, edge, pick, pool_here = call(
        pick_kernel,
        [
            (NSRC,) + pool.shape[1:],
            ((4 + 2 * held) * h + 1, gx, gy),
            (NSRC, held, 8, gy),
            pool.shape,
        ],
        [HBM] * 4,
        [pltpu.SMEM(source_index.shape, jnp.int32), pltpu.SemaphoreType.DMA((6,))],
        moved=4 << 20,
    )(*[
        pltpu.with_memory_space_constraint(x, pltpu.HBM)
        for x in (source_index, pool, metric, screening)
    ])
    keep, send, edge = call(
        gather_kernel,
        [(NSRC, h, gx, gy)] * 2 + [edge.shape],
        [VMEM] * 5,
        alias={4: 2},
    )(own, pick, pool_here, theirs, edge)
    near = to_slab(edge)
    part = keep
    for step in range(len(bits)):
        low, high = (bits[0], bits[-1]) if step == 0 else (bits[-1 - step], bits[step])
        swap = 1 if step == 0 else 0
        across = among(lambda o, z: (o ^ swap ^ (high if o % 2 else low), z))
        merge = call(merge_kernel, [part.shape], [VMEM] * 2, flops=0 if step else HINT)
        (part,) = merge(part, across(send if step == 0 else part))
    halo = to_slab_all(part)
    last = (4 + held) * h + 1
    cuts = [last * i // PIECES for i in range(PIECES + 1)]
    far = jnp.concatenate([to_sibling(near[a:b]) for a, b in zip(cuts, cuts[1:])], axis=0)
    total = planes + 2 * h
    coef, scaled = call(
        coefficient_kernel,
        [(6, total * gx, gy), (total * gx, gy)],
        [SMEM] + [VMEM] * 5,
        [pltpu.VMEM((total, gx, gy), jnp.float32)] * 2
        + [pltpu.VMEM((total + 1, gx, gy), jnp.float32)]
        + [pltpu.VMEM((total, gx, gy), jnp.float32)] * 2,
        moved=0,
    )(target_row, pool_here, metric, screening, near, far)
    halo, coef, scaled = lax.optimization_barrier((halo, coef, scaled))
    kept = planes - h
    lacks = jnp.where(
        side == 0,
        jnp.concatenate([halo, part[:, :kept]], axis=1),
        jnp.concatenate([part[:, h - kept :], halo], axis=1),
    )
    sibling = to_sibling(lacks)
    count = 2 * h
    own_field = pltpu.VMEM((NSRC, count * gx, gy), jnp.float32)
    (level,) = call(
        functools.partial(early_kernel, weights),
        [(SWEEPS - 2, NSRC, count * gx, gy)],
        [VMEM] * 4,
        [own_field] * 3,
    )(coef, scaled, part, halo)
    field = pltpu.VMEM((NSRC, total * gx, gy), jnp.float32)
    (out,) = call(
        functools.partial(sweep_kernel, weights),
        [(1, planes, gx, gy)],
        [VMEM] * 6,
        [field] * 2 + [pltpu.VMEM((SWEEPS - 1, NSRC, total * gx, gy), jnp.float32)],
    )(coef, scaled, part, halo, sibling, level)
    return out


def solution(mesh):
    in_specs = (
        P("orb", "slab", None, None),
        P("orb"),
        P(),
        P(None, "slab", None, None),
        P("slab", None, None),
    )
    out_specs = P("orb", "slab", None, None)
    return jax.shard_map(shards, mesh=mesh, in_specs=in_specs, out_specs=out_specs, check_vma=False)
```

```python
import functools
import math

import jax
import jax.numpy as jnp
from jax import lax
from jax.experimental import pallas as pl
from jax.experimental.pallas import tpu as pltpu
from jax.sharding import PartitionSpec as P

NSRC = 3
SWEEPS = 6
HALO = SWEEPS - 1
AXES = ("orb", "slab")
HINT = 10**10
PIECES = 4
VMEM = pl.BlockSpec(memory_space=pltpu.VMEM)
SMEM = pl.BlockSpec(memory_space=pltpu.SMEM)
HBM = pl.BlockSpec(memory_space=pltpu.HBM)


def step_sizes(count):
    return [
        1.0 / (1.025 + 0.975 * math.cos(math.pi * (2 * k + 1) / (2 * count))) for k in range(count)
    ]


def upper_side():
    return 1 - lax.rem(lax.axis_index("orb"), 2)


def call(kernel, out_shapes, in_specs, scratch=(), flops=0, moved=0, alias=None):
    return pl.pallas_call(
        kernel,
        out_shape=[jax.ShapeDtypeStruct(s, jnp.float32) for s in out_shapes],
        in_specs=in_specs,
        out_specs=[VMEM] * len(out_shapes),
        scratch_shapes=list(scratch),
        compiler_params=pltpu.CompilerParams(vmem_limit_bytes=16 << 20),
        input_output_aliases=alias or {},
        cost_estimate=pl.CostEstimate(flops=flops, transcendentals=0, bytes_accessed=moved),
    )


def pick_kernel(
    index_hbm, pool_hbm, metric_hbm, screening_hbm, own, edge, pick, pool, index, screen, face, sems
):
    h = HALO
    held, planes, gx, gy = pool.shape
    orb = lax.axis_index("orb")
    side = upper_side()
    sibling = orb - 1 + 2 * side
    mine = side * (planes - h)
    parts = [
        (index_hbm, index),
        (pool_hbm, pool),
        (screening_hbm.at[pl.ds(mine, h)], screen),
        (metric_hbm.at[0, pl.ds(mine, h)], face.at[0, pl.ds(1, h)]),
        (metric_hbm.at[1, pl.ds(mine, h)], face.at[1, pl.ds(1, h)]),
        (
            metric_hbm.at[2, pl.ds(side * (planes - h - 1), h + 1)],
            face.at[2, pl.ds(1 - side, h + 1)],
        ),
    ]
    copies = [pltpu.make_async_copy(a, b, sems.at[i]) for i, (a, b) in enumerate(parts)]
    for copy in copies:
        copy.start()
    for copy in copies[:2]:
        copy.wait()
    for s in range(NSRC):
        group, place = index[s] // held, lax.rem(index[s], held)
        own[s] = jnp.where(group == orb, pool[place], 0.0)
        for r in range(held):
            there = jnp.logical_and(group == sibling, place == r)
            pick[s, r] = jnp.where(there, jnp.ones(pick.shape[2:], jnp.float32), 0.0)
    rest = (edge.shape[0] - 4 * h + 2,) + edge.shape[1:]
    edge[pl.ds(4 * h - 2, rest[0])] = jnp.zeros(rest, jnp.float32)
    for copy in copies[2:]:
        copy.wait()
    x_id = lax.broadcasted_iota(jnp.int32, (gx, gy), 0)
    y_id = lax.broadcasted_iota(jnp.int32, (gx, gy), 1)
    for i in range(h):
        x_hi, y_hi, z_hi = face[0, i + 1], face[1, i + 1], face[2, i + 1]
        z_lo = face[2, i] if i else jnp.where(side == 0, 0.0, face[2, i])
        x_lo = jnp.where(x_id == 0, 0.0, pltpu.roll(x_hi, 1, 0))
        y_lo = jnp.where(y_id == 0, 0.0, pltpu.roll(y_hi, 1, 1))
        edge[i] = screen[i] + z_hi + z_lo + x_hi + x_lo + y_hi + y_lo
        edge[h + i] = z_hi
    edge[2 * h : 3 * h - 1] = face[0, pl.ds(1 + side, h - 1)]
    edge[3 * h - 1 : 4 * h - 2] = face[1, pl.ds(1 + side, h - 1)]


def gather_kernel(own, pick, pool, theirs, blank, keep, send, edge):
    del blank
    h = HALO
    held, planes, gx = pool.shape[:3]
    side = upper_side()
    mine = side * (planes - h)
    for part, start in ((send, (1 - side) * (planes - h)), (keep, mine)):
        for s in range(NSRC):
            total = own[s, pl.ds(start, h)]
            for r in range(held):
                factor = jnp.tile(pick[s, r], (gx // pick.shape[2], 1))
                total += factor * theirs[r, pl.ds(start, h)]
            part[s] = total
    for r in range(held):
        edge[pl.ds((4 + r) * h - 2, h)] = pool[r, pl.ds(mine, h)]
        edge[pl.ds((4 + held + r) * h - 2, h)] = theirs[r, pl.ds(mine, h)]


def merge_kernel(mine, theirs, both):
    both[...] = mine[...] + theirs[...]


def coefficient_kernel(
    row, pool, metric, screening, near, far, coef, scaled, fx, fy, fz, scr, tgt
):
    side = upper_side()
    slab, slabs = lax.axis_index("slab"), lax.axis_size("slab")
    planes, gx, gy = screening.shape
    total = planes + 2 * HALO
    lower = side * (HALO + planes)
    upper = (1 - side) * (HALO + planes)
    h = HALO
    held = pool.shape[0]
    near_row = (4 + held + row[0]) * h - 2
    far_row = (4 + row[0]) * h - 2
    blank = jnp.zeros((gx, gy), jnp.float32)
    for e in (0, total - 1):
        fx[e] = blank
        fy[e] = blank
    fz[0] = blank
    for halo, at, inner, above, own_slot in (
        (near, lower, lower + 1 - side, lower + 1, near_row),
        (far, upper, upper + side, upper + 1, far_row),
    ):
        scr[pl.ds(at, h)] = halo[0:h]
        fz[pl.ds(above, h)] = halo[h : 2 * h]
        fx[pl.ds(inner, h - 1)] = halo[2 * h : 3 * h - 1]
        fy[pl.ds(inner, h - 1)] = halo[3 * h - 1 : 4 * h - 2]
        tgt[pl.ds(at, h)] = halo[pl.ds(own_slot, h)]
    fz[h + 1 : h + 1 + planes] = metric[2]
    scr[h : h + planes] = screening[...]
    fx[h : h + planes] = metric[0]
    fy[h : h + planes] = metric[1]
    tgt[h : h + planes] = pool[row[0]]
    first = jnp.where(slab == 0, h, 0)
    last = jnp.where(slab == slabs - 1, h + planes, total)
    x_id = lax.broadcasted_iota(jnp.int32, (gx, gy), 0)
    y_id = lax.broadcasted_iota(jnp.int32, (gx, gy), 1)

    @pl.loop(0, total, unroll=6)
    def _(e):
        z_hi, z_lo = fz[e + 1], fz[e]
        x_hi, y_hi = fx[e], fy[e]
        x_lo = jnp.where(x_id == 0, 0.0, pltpu.roll(x_hi, 1, 0))
        y_lo = jnp.where(y_id == 0, 0.0, pltpu.roll(y_hi, 1, 1))
        here = jnp.logical_and(e >= h, e < h + planes)
        rest = jnp.where(e == h + planes, z_lo, 0.0)
        diag = scr[e] + jnp.where(here, z_hi + z_lo + x_hi + x_lo + y_hi + y_lo, rest)
        inside = jnp.logical_and(e >= first, e < last)
        inverse = 1.0 / jnp.where(inside, diag, 1.0)
        inverse = jnp.where(inside, inverse, 0.0)
        rows = pl.ds(pl.multiple_of(e * gx, gx), gx)
        coef[0, rows] = z_hi * inverse
        coef[1, rows] = z_lo * inverse
        coef[2, rows] = jnp.where(x_id == gx - 1, 0.0, x_hi * inverse)
        coef[3, rows] = x_lo * inverse
        coef[4, rows] = jnp.where(y_id == gy - 1, 0.0, y_hi * inverse)
        coef[5, rows] = y_lo * inverse
        scaled[rows] = tgt[e] * inverse


SOURCE, DENSITY, START = 0, 1, 2


def take_planes(weight, scaled, state, part, at):
    count, gx, gy = part.shape[1:]
    for i in range(count):
        rows = pl.ds(pl.multiple_of((at + i) * gx, gx), gx)
        t = scaled[rows]
        for s in range(NSRC):
            cells = part[s, i]
            b = t * cells
            state[SOURCE, s, rows] = cells
            state[DENSITY, s, rows] = b
            state[START, s, rows] = weight * b


def sweep_planes(k, weight, coef, state, begin, count, gx, out=None, shift=0):
    gy = state.shape[-1]
    old = START + k - 1

    @pl.loop(0, count, unroll=count)
    def _(i):
        for j in range(0, gx, 8):
            at = pl.multiple_of((begin + i) * gx, gx) + j
            here = pl.ds(at, 8)
            c = [coef[n, here] for n in range(6)]
            acc = None
            for s in range(NSRC):
                v = state[old, s, here]
                total = state[DENSITY, s, here]
                total += c[0] * state[old, s, pl.ds(at + gx, 8)]
                total += c[1] * state[old, s, pl.ds(at - gx, 8)]
                total += c[2] * state[old, s, pl.ds(at + 1, 8)]
                total += c[3] * state[old, s, pl.ds(at - 1, 8)]
                total += c[4] * pltpu.roll(v, gy - 1, 1)
                total += c[5] * pltpu.roll(v, 1, 1)
                v = (1.0 - weight) * v + weight * total
                if out is None:
                    state[old + 1, s, here] = v
                else:
                    term = v * state[SOURCE, s, here]
                    acc = term if acc is None else acc + term
            if out is not None:
                out[begin + i - shift, j : j + 8] = acc


def inner_kernel(weights, coef, scaled, middle, inner, state):
    side = upper_side()
    h = HALO
    gx = middle.shape[2]
    extra, rest = middle.shape[1], inner.shape[1]
    planes = extra + rest
    take_planes(weights[0], scaled, state, middle, h + side * rest)
    take_planes(weights[0], scaled, state, inner, h + (1 - side) * extra)
    for k in range(1, SWEEPS):
        if planes > 2 * k:
            sweep_planes(k, weights[k], coef, state, h + k, planes - 2 * k, gx)


def near_kernel(weights, coef, scaled, halo, known, state, early):
    del known
    side = upper_side()
    h = HALO
    gx = halo.shape[2]
    total = state.shape[2] // gx
    planes = total - 2 * h
    take_planes(weights[0], scaled, state, halo, side * (h + planes))
    for k in range(1, SWEEPS):
        count = min(h, h + planes - 2 * k)
        begin = jnp.where(side == 0, k, total - k - count)
        if k < SWEEPS - 1:
            sweep_planes(k, weights[k], coef, state, begin, count, gx)
        else:
            sweep_planes(k, weights[k], coef, state, begin, count, gx, early, begin)


def far_kernel(weights, coef, scaled, halo, known, early, state, out):
    del known
    side = upper_side()
    h = HALO
    gx = halo.shape[2]
    planes = out.shape[1]
    total = planes + 2 * h
    take_planes(weights[0], scaled, state, halo, (1 - side) * (h + planes))
    for k in range(1, SWEEPS):
        begin = jnp.where(side == 0, h + planes - k, k)
        if k < SWEEPS - 1:
            sweep_planes(k, weights[k], coef, state, begin, h, gx)
        else:
            sweep_planes(k, weights[k], coef, state, begin, h, gx, out.at[0], h)
    done = early.shape[0]
    out[0, pl.ds(side * (planes - done), done)] = early[...]


def shards(pool, target_row, source_index, metric, screening):
    held, planes, gx, gy = pool.shape
    n_orb, n_slab = lax.axis_size("orb"), lax.axis_size("slab")
    h = HALO
    weights = step_sizes(SWEEPS)
    side = upper_side()

    def place(o, z):
        return o * n_slab + z

    def among(moved):
        pairs = [
            (place(o, z), place(*moved(o, z)))
            for o in range(n_orb)
            for z in range(n_slab)
            if 0 <= moved(o, z)[1] < n_slab
        ]
        return lambda x: lax.ppermute(x, AXES, pairs)

    to_sibling = among(lambda o, z: (o ^ 1, z))
    to_slab = among(lambda o, z: (o ^ 1, z - 1 if o % 2 else z + 1))

    def next_slab(o, z):
        there = z - 1 if o % 2 else z + 1
        return (o ^ 1, there) if 0 <= there < n_slab else (o ^ 2, z)

    to_slab_all = among(next_slab)
    bits = [1 << b for b in range(1, n_orb.bit_length() - 1)]

    theirs = to_sibling(pool)
    own, edge, pick, pool_here = call(
        pick_kernel,
        [
            (NSRC,) + pool.shape[1:],
            ((4 + 2 * held) * h - 2, gx, gy),
            (NSRC, held, 8, gy),
            pool.shape,
        ],
        [HBM] * 4,
        [
            pltpu.SMEM(source_index.shape, jnp.int32),
            pltpu.VMEM((h, gx, gy), jnp.float32),
            pltpu.VMEM((3, h + 2, gx, gy), jnp.float32),
            pltpu.SemaphoreType.DMA((6,)),
        ],
        moved=4 << 20,
    )(*[
        pltpu.with_memory_space_constraint(x, pltpu.HBM)
        for x in (source_index, pool, metric, screening)
    ])
    keep, send, edge = call(
        gather_kernel,
        [(NSRC, h, gx, gy)] * 2 + [edge.shape],
        [VMEM] * 5,
        alias={4: 2},
    )(own, pick, pool_here, theirs, edge)
    near = to_slab(edge)
    part = keep
    for step in range(len(bits)):
        low, high = (bits[0], bits[-1]) if step == 0 else (bits[-1 - step], bits[step])
        swap = 1 if step == 0 else 0
        across = among(lambda o, z: (o ^ swap ^ (high if o % 2 else low), z))
        merge = call(merge_kernel, [part.shape], [VMEM] * 2, flops=0 if step else HINT)
        (part,) = merge(part, across(send if step == 0 else part))
    halo = to_slab_all(part)
    last = (4 + held) * h - 2
    cuts = [last * i // PIECES for i in range(PIECES + 1)]
    far = jnp.concatenate([to_sibling(near[a:b]) for a, b in zip(cuts, cuts[1:])], axis=0)
    total = planes + 2 * h
    coef, scaled = call(
        coefficient_kernel,
        [(6, total * gx, gy), (total * gx, gy)],
        [SMEM] + [VMEM] * 5,
        [pltpu.VMEM((total, gx, gy), jnp.float32)] * 2
        + [pltpu.VMEM((total + 1, gx, gy), jnp.float32)]
        + [pltpu.VMEM((total, gx, gy), jnp.float32)] * 2,
        moved=0,
    )(target_row, pool_here, metric, screening, near, far)
    rest = planes - h
    inner = to_sibling(lax.dynamic_slice_in_dim(part, side * (h - rest), rest, axis=1))
    (state,) = call(
        functools.partial(inner_kernel, weights),
        [(START + SWEEPS - 1, NSRC, total * gx, gy)],
        [VMEM] * 4,
    )(coef, scaled, part, inner)
    halo, state, coef, scaled = lax.optimization_barrier((halo, state, coef, scaled))
    state, early = call(
        functools.partial(near_kernel, weights),
        [state.shape, (rest, gx, gy)],
        [VMEM] * 4,
        alias={3: 0},
    )(coef, scaled, halo, state)
    state, out = call(
        functools.partial(far_kernel, weights),
        [state.shape, (1, planes, gx, gy)],
        [VMEM] * 5,
        alias={3: 0},
    )(coef, scaled, to_sibling(halo), state, early)
    return out


def solution(mesh):
    in_specs = (
        P("orb", "slab", None, None),
        P("orb"),
        P(),
        P(None, "slab", None, None),
        P("slab", None, None),
    )
    out_specs = P("orb", "slab", None, None)
    return jax.shard_map(shards, mesh=mesh, in_specs=in_specs, out_specs=out_specs, check_vma=False)
```

```python
import functools
import math

import jax
import jax.numpy as jnp
from jax import lax
from jax.experimental import pallas as pl
from jax.experimental.pallas import tpu as pltpu
from jax.sharding import PartitionSpec as P

NSRC = 3
SWEEPS = 6
HALO = SWEEPS - 1
AXES = ("orb", "slab")
HINT = 10**10
PIECES = 4
VMEM = pl.BlockSpec(memory_space=pltpu.VMEM)
SMEM = pl.BlockSpec(memory_space=pltpu.SMEM)
HBM = pl.BlockSpec(memory_space=pltpu.HBM)


def step_sizes(count):
    return [
        1.0 / (1.025 + 0.975 * math.cos(math.pi * (2 * k + 1) / (2 * count))) for k in range(count)
    ]


def upper_side():
    return 1 - lax.rem(lax.axis_index("orb"), 2)


def on_each_side(body):
    side = upper_side()
    for constant in (0, 1):
        pl.when(side == constant)(functools.partial(body, constant))


def call(kernel, out_shapes, in_specs, scratch=(), flops=0, moved=0, alias=None):
    return pl.pallas_call(
        kernel,
        out_shape=[jax.ShapeDtypeStruct(s, jnp.float32) for s in out_shapes],
        in_specs=in_specs,
        out_specs=[VMEM] * len(out_shapes),
        scratch_shapes=list(scratch),
        compiler_params=pltpu.CompilerParams(vmem_limit_bytes=16 << 20),
        input_output_aliases=alias or {},
        cost_estimate=pl.CostEstimate(flops=flops, transcendentals=0, bytes_accessed=moved),
    )


def pick_kernel(
    index_hbm, pool_hbm, metric_hbm, screening_hbm, own, edge, pick, pool, index, screen, face, sems
):
    h = HALO
    held, planes, gx, gy = pool.shape
    orb = lax.axis_index("orb")
    side = upper_side()
    sibling = orb - 1 + 2 * side
    mine = side * (planes - h)
    parts = [
        (index_hbm, index),
        (pool_hbm, pool),
        (screening_hbm.at[pl.ds(mine, h)], screen),
        (metric_hbm.at[0, pl.ds(mine, h)], face.at[0, pl.ds(1, h)]),
        (metric_hbm.at[1, pl.ds(mine, h)], face.at[1, pl.ds(1, h)]),
        (
            metric_hbm.at[2, pl.ds(side * (planes - h - 1), h + 1)],
            face.at[2, pl.ds(1 - side, h + 1)],
        ),
    ]
    copies = [pltpu.make_async_copy(a, b, sems.at[i]) for i, (a, b) in enumerate(parts)]
    for copy in copies:
        copy.start()
    for copy in copies[:2]:
        copy.wait()
    for s in range(NSRC):
        group, place = index[s] // held, lax.rem(index[s], held)
        own[s] = jnp.where(group == orb, pool[place], 0.0)
        for r in range(held):
            there = jnp.logical_and(group == sibling, place == r)
            pick[s, r] = jnp.where(there, jnp.ones(pick.shape[2:], jnp.float32), 0.0)
    rest = (edge.shape[0] - 4 * h + 2,) + edge.shape[1:]
    edge[pl.ds(4 * h - 2, rest[0])] = jnp.zeros(rest, jnp.float32)
    for copy in copies[2:]:
        copy.wait()
    x_id = lax.broadcasted_iota(jnp.int32, (gx, gy), 0)
    y_id = lax.broadcasted_iota(jnp.int32, (gx, gy), 1)
    for i in range(h):
        x_hi, y_hi, z_hi = face[0, i + 1], face[1, i + 1], face[2, i + 1]
        z_lo = face[2, i] if i else jnp.where(side == 0, 0.0, face[2, i])
        x_lo = jnp.where(x_id == 0, 0.0, pltpu.roll(x_hi, 1, 0))
        y_lo = jnp.where(y_id == 0, 0.0, pltpu.roll(y_hi, 1, 1))
        edge[i] = screen[i] + z_hi + z_lo + x_hi + x_lo + y_hi + y_lo
        edge[h + i] = z_hi
    edge[2 * h : 3 * h - 1] = face[0, pl.ds(1 + side, h - 1)]
    edge[3 * h - 1 : 4 * h - 2] = face[1, pl.ds(1 + side, h - 1)]


def gather_kernel(own, pick, pool, theirs, blank, keep, send, edge):
    del blank
    h = HALO
    held, planes, gx = pool.shape[:3]
    side = upper_side()
    mine = side * (planes - h)
    for part, start in ((send, (1 - side) * (planes - h)), (keep, mine)):
        for s in range(NSRC):
            total = own[s, pl.ds(start, h)]
            for r in range(held):
                factor = jnp.tile(pick[s, r], (gx // pick.shape[2], 1))
                total += factor * theirs[r, pl.ds(start, h)]
            part[s] = total
    for r in range(held):
        edge[pl.ds((4 + r) * h - 2, h)] = pool[r, pl.ds(mine, h)]
        edge[pl.ds((4 + held + r) * h - 2, h)] = theirs[r, pl.ds(mine, h)]


def merge_kernel(mine, theirs, both):
    both[...] = mine[...] + theirs[...]


def coefficient_kernel(
    row, pool, metric, screening, near, far, coef, scaled, fx, fy, fz, scr, tgt
):
    side = upper_side()
    slab, slabs = lax.axis_index("slab"), lax.axis_size("slab")
    planes, gx, gy = screening.shape
    total = planes + 2 * HALO
    lower = side * (HALO + planes)
    upper = (1 - side) * (HALO + planes)
    h = HALO
    held = pool.shape[0]
    near_row = (4 + held + row[0]) * h - 2
    far_row = (4 + row[0]) * h - 2
    blank = jnp.zeros((gx, gy), jnp.float32)
    for e in (0, total - 1):
        fx[e] = blank
        fy[e] = blank
    fz[0] = blank
    for halo, at, inner, above, own_slot in (
        (near, lower, lower + 1 - side, lower + 1, near_row),
        (far, upper, upper + side, upper + 1, far_row),
    ):
        scr[pl.ds(at, h)] = halo[0:h]
        fz[pl.ds(above, h)] = halo[h : 2 * h]
        fx[pl.ds(inner, h - 1)] = halo[2 * h : 3 * h - 1]
        fy[pl.ds(inner, h - 1)] = halo[3 * h - 1 : 4 * h - 2]
        tgt[pl.ds(at, h)] = halo[pl.ds(own_slot, h)]
    fz[h + 1 : h + 1 + planes] = metric[2]
    scr[h : h + planes] = screening[...]
    fx[h : h + planes] = metric[0]
    fy[h : h + planes] = metric[1]
    tgt[h : h + planes] = pool[row[0]]
    first = jnp.where(slab == 0, h, 0)
    last = jnp.where(slab == slabs - 1, h + planes, total)
    x_id = lax.broadcasted_iota(jnp.int32, (gx, gy), 0)
    y_id = lax.broadcasted_iota(jnp.int32, (gx, gy), 1)

    @pl.loop(0, total, unroll=6)
    def _(e):
        z_hi, z_lo = fz[e + 1], fz[e]
        x_hi, y_hi = fx[e], fy[e]
        x_lo = jnp.where(x_id == 0, 0.0, pltpu.roll(x_hi, 1, 0))
        y_lo = jnp.where(y_id == 0, 0.0, pltpu.roll(y_hi, 1, 1))
        here = jnp.logical_and(e >= h, e < h + planes)
        rest = jnp.where(e == h + planes, z_lo, 0.0)
        diag = scr[e] + jnp.where(here, z_hi + z_lo + x_hi + x_lo + y_hi + y_lo, rest)
        inside = jnp.logical_and(e >= first, e < last)
        inverse = 1.0 / jnp.where(inside, diag, 1.0)
        inverse = jnp.where(inside, inverse, 0.0)
        rows = pl.ds(pl.multiple_of(e * gx, gx), gx)
        coef[0, rows] = z_hi * inverse
        coef[1, rows] = z_lo * inverse
        coef[2, rows] = jnp.where(x_id == gx - 1, 0.0, x_hi * inverse)
        coef[3, rows] = x_lo * inverse
        coef[4, rows] = jnp.where(y_id == gy - 1, 0.0, y_hi * inverse)
        coef[5, rows] = y_lo * inverse
        scaled[rows] = tgt[e] * inverse


SOURCE, DENSITY, START = 0, 1, 2


def take_planes(weight, scaled, state, part, at):
    count, gx, gy = part.shape[1:]
    for i in range(count):
        first = (at + i) * gx
        rows = pl.ds(first if isinstance(at, int) else pl.multiple_of(first, gx), gx)
        t = scaled[rows]
        for s in range(NSRC):
            cells = part[s, i]
            b = t * cells
            state[SOURCE, s, rows] = cells
            state[DENSITY, s, rows] = b
            state[START, s, rows] = weight * b


def sweep_planes(k, weight, coef, state, begin, count, gx, out=None, shift=0):
    gy = state.shape[-1]
    old = START + k - 1

    for i in range(count):
        for j in range(0, gx, 8):
            at = (begin + i) * gx + j
            if not isinstance(begin, int):
                at = pl.multiple_of(at, 8)
            here = pl.ds(at, 8)
            c = [coef[n, here] for n in range(6)]
            acc = None
            for s in range(NSRC):
                v = state[old, s, here]
                total = state[DENSITY, s, here]
                total += c[0] * state[old, s, pl.ds(at + gx, 8)]
                total += c[1] * state[old, s, pl.ds(at - gx, 8)]
                total += c[2] * state[old, s, pl.ds(at + 1, 8)]
                total += c[3] * state[old, s, pl.ds(at - 1, 8)]
                total += c[4] * pltpu.roll(v, gy - 1, 1)
                total += c[5] * pltpu.roll(v, 1, 1)
                v = (1.0 - weight) * v + weight * total
                if out is None:
                    state[old + 1, s, here] = v
                else:
                    term = v * state[SOURCE, s, here]
                    acc = term if acc is None else acc + term
            if out is not None:
                out[begin + i - shift, j : j + 8] = acc


def inner_kernel(weights, coef, scaled, middle, inner, state):
    side = upper_side()
    h = HALO
    gx = middle.shape[2]
    extra, rest = middle.shape[1], inner.shape[1]
    planes = extra + rest
    take_planes(weights[0], scaled, state, middle, h + side * rest)
    take_planes(weights[0], scaled, state, inner, h + (1 - side) * extra)
    for k in range(1, SWEEPS):
        if planes > 2 * k:
            sweep_planes(k, weights[k], coef, state, h + k, planes - 2 * k, gx)


def near_kernel(weights, coef, scaled, halo, known, state, early):
    del known
    h = HALO
    gx = halo.shape[2]
    total = state.shape[2] // gx
    planes = total - 2 * h

    @on_each_side
    def _(side):
        take_planes(weights[0], scaled, state, halo, side * (h + planes))
        for k in range(1, SWEEPS):
            count = min(h, h + planes - 2 * k)
            begin = k if side == 0 else total - k - count
            if k < SWEEPS - 1:
                sweep_planes(k, weights[k], coef, state, begin, count, gx)
            else:
                sweep_planes(k, weights[k], coef, state, begin, count, gx, early, begin)


def far_kernel(weights, coef, scaled, halo, known, early, state, out):
    del known
    h = HALO
    gx = halo.shape[2]
    planes = out.shape[1]
    done = early.shape[0]

    @on_each_side
    def _(side):
        take_planes(weights[0], scaled, state, halo, (1 - side) * (h + planes))
        out[0, pl.ds(side * (planes - done), done)] = early[...]
        for k in range(1, SWEEPS):
            begin = k if side else h + planes - k
            if k < SWEEPS - 1:
                sweep_planes(k, weights[k], coef, state, begin, h, gx)
            else:
                sweep_planes(k, weights[k], coef, state, begin, h, gx, out.at[0], h)


def shards(pool, target_row, source_index, metric, screening):
    held, planes, gx, gy = pool.shape
    n_orb, n_slab = lax.axis_size("orb"), lax.axis_size("slab")
    h = HALO
    weights = step_sizes(SWEEPS)
    side = upper_side()

    def place(o, z):
        return o * n_slab + z

    def among(moved):
        pairs = [
            (place(o, z), place(*moved(o, z)))
            for o in range(n_orb)
            for z in range(n_slab)
            if 0 <= moved(o, z)[1] < n_slab
        ]
        return lambda x: lax.ppermute(x, AXES, pairs)

    to_sibling = among(lambda o, z: (o ^ 1, z))
    to_slab = among(lambda o, z: (o ^ 1, z - 1 if o % 2 else z + 1))

    def next_slab(o, z):
        there = z - 1 if o % 2 else z + 1
        return (o ^ 1, there) if 0 <= there < n_slab else (o ^ 2, z)

    to_slab_all = among(next_slab)
    bits = [1 << b for b in range(1, n_orb.bit_length() - 1)]

    theirs = to_sibling(pool)
    own, edge, pick, pool_here = call(
        pick_kernel,
        [
            (NSRC,) + pool.shape[1:],
            ((4 + 2 * held) * h - 2, gx, gy),
            (NSRC, held, 8, gy),
            pool.shape,
        ],
        [HBM] * 4,
        [
            pltpu.SMEM(source_index.shape, jnp.int32),
            pltpu.VMEM((h, gx, gy), jnp.float32),
            pltpu.VMEM((3, h + 2, gx, gy), jnp.float32),
            pltpu.SemaphoreType.DMA((6,)),
        ],
        moved=4 << 20,
    )(*[
        pltpu.with_memory_space_constraint(x, pltpu.HBM)
        for x in (source_index, pool, metric, screening)
    ])
    keep, send, edge = call(
        gather_kernel,
        [(NSRC, h, gx, gy)] * 2 + [edge.shape],
        [VMEM] * 5,
        alias={4: 2},
    )(own, pick, pool_here, theirs, edge)
    near = to_slab(edge)
    part = keep
    for step in range(len(bits)):
        low, high = (bits[0], bits[-1]) if step == 0 else (bits[-1 - step], bits[step])
        swap = 1 if step == 0 else 0
        across = among(lambda o, z: (o ^ swap ^ (high if o % 2 else low), z))
        merge = call(merge_kernel, [part.shape], [VMEM] * 2, flops=0 if step else HINT)
        (part,) = merge(part, across(send if step == 0 else part))
    halo = to_slab_all(part)
    last = (4 + held) * h - 2
    cuts = [last * i // PIECES for i in range(PIECES + 1)]
    far = jnp.concatenate([to_sibling(near[a:b]) for a, b in zip(cuts, cuts[1:])], axis=0)
    total = planes + 2 * h
    coef, scaled = call(
        coefficient_kernel,
        [(6, total * gx, gy), (total * gx, gy)],
        [SMEM] + [VMEM] * 5,
        [pltpu.VMEM((total, gx, gy), jnp.float32)] * 2
        + [pltpu.VMEM((total + 1, gx, gy), jnp.float32)]
        + [pltpu.VMEM((total, gx, gy), jnp.float32)] * 2,
        moved=0,
    )(target_row, pool_here, metric, screening, near, far)
    rest = planes - h
    inner = to_sibling(lax.dynamic_slice_in_dim(part, side * (h - rest), rest, axis=1))
    (state,) = call(
        functools.partial(inner_kernel, weights),
        [(START + SWEEPS - 1, NSRC, total * gx, gy)],
        [VMEM] * 4,
    )(coef, scaled, part, inner)
    halo, state, coef, scaled = lax.optimization_barrier((halo, state, coef, scaled))
    state, early = call(
        functools.partial(near_kernel, weights),
        [state.shape, (rest, gx, gy)],
        [VMEM] * 4,
        alias={3: 0},
    )(coef, scaled, halo, state)
    state, out = call(
        functools.partial(far_kernel, weights),
        [state.shape, (1, planes, gx, gy)],
        [VMEM] * 5,
        alias={3: 0},
    )(coef, scaled, to_sibling(halo), state, early)
    return out


def solution(mesh):
    in_specs = (
        P("orb", "slab", None, None),
        P("orb"),
        P(),
        P(None, "slab", None, None),
        P("slab", None, None),
    )
    out_specs = P("orb", "slab", None, None)
    return jax.shard_map(shards, mesh=mesh, in_specs=in_specs, out_specs=out_specs, check_vma=False)
```
